32 devices in a mesh: slab: 8 (over z, y), rep: 4 (over x, core).
Axes of the slice: x: 2, y: 2, z: 4, core: 2. Of those that a mesh axis runs over, the one named last changes fastest.
Arguments:
- feats: bfloat16 [32768, 128], P(('slab', 'rep')), may hold values from -6 to 6
- cotangent: bfloat16 [32768, 128], P(('slab', 'rep')), may hold values from -6 to 6
- tile_table: bfloat16 [2048, 128, 128], P(('slab', 'rep')), as said below
- edge_src: int32 [32, 256], P(('slab', 'rep')), may hold values from 0 to 31
- edge_tile: int32 [32, 256], P(('slab', 'rep')), may hold values from 0 to 63
- edge_slot: int32 [32, 256], P(('slab', 'rep')), may hold values from 0 to 63
- edge_count: int32 [32], P(('slab', 'rep')), may hold values from 32 to 256, as said below
- slot_block: int32 [8, 64], replicated, may hold values from 0 to 31
- norm_gain: float32 [256], replicated, may hold values from 0.1 to 1.9
- w_in: bfloat16 [256, 512], replicated, may hold values from -0.375 to 0.375
- b_in: float32 [512], replicated, may hold values from -3 to 3
- w_out: bfloat16 [512, 128], replicated, may hold values from -0.25 to 0.25
Outputs:
- updated: bfloat16 [32768, 128], P(('slab', 'rep'))
- grad_feats: float32 [32768, 128], P(('slab', 'rep'))
- grad_gain: float32 [256], replicated
- grad_w_in: float32 [256, 512], replicated
- grad_b_in: float32 [512], replicated
- grad_w_out: float32 [512, 128], replicated
The draws below stay inside these ranges and needn't reach their ends.
Inputs may be any that keep to these rules, and one draw needn't show every extreme that they name: `edge_count`: some device uses all 256 entries and some only 32. `tile_table`: entries are zero or a positive edge weight.
All inputs are finite; a program needn't handle non-finite values.
Results may differ from the reference program's by a relative error of at most 0.0061.
Values may be sent and summed in bfloat16 or wider, within the bound.
A program may use at most 64 MiB of HBM per device.

```python
import jax
import jax.numpy as jnp
from jax import lax

W = 128
HID = 512
B = 128
NEIGH = 8
SLOT_CAP = 8
BLK_DEV = 8
EB = 256
TILE_DEV = 64
BLK_SLAB = 32
SLOTS = 64
DEV_COUNT = 32
NODES = 32768
TILES = 2048
N_SLAB = 8
N_REP = 4


def draw_tile_table(key, part):
    shape = (TILES, B, B)
    keep = jax.random.bernoulli(jax.random.fold_in(key, 1), min(0.5, 1.5 / B), shape)
    level = jax.random.uniform(jax.random.fold_in(key, 2), shape, jnp.float32)
    weights = 0.15 + 0.35 * level
    scaled = jnp.where(keep, weights, 0.0)
    return scaled.astype(jnp.float32).astype(jnp.bfloat16)


def draw_edge_count(key, part):
    least = EB // 8
    extent = EB - least
    rolled = jax.random.randint(jax.random.fold_in(key, 11), (DEV_COUNT,), 0, extent + 1)
    counts = least + rolled * rolled * rolled // max(extent * extent, 1)
    chosen = jax.random.randint(jax.random.fold_in(key, 12), (2,), 0, DEV_COUNT)
    busiest = chosen[0]
    lightest = (chosen[0] + 1 + chosen[1] % (DEV_COUNT - 1)) % DEV_COUNT
    device_ids = jnp.arange(DEV_COUNT)
    counts = jnp.where(device_ids == busiest, EB, counts)
    counts = jnp.where(device_ids == lightest, least, counts)
    return counts.astype(jnp.int32)


def touch_ends(drawn, own_key, low, largest):
    place = [jax.random.randint(jax.random.fold_in(own_key, axis), (), 0, length) for axis, length in enumerate(drawn.shape)]
    widest = drawn.shape.index(max(drawn.shape))
    beside = place[:widest] + [(place[widest] + 1) % drawn.shape[widest]] + place[widest + 1:]
    return drawn.at[tuple(place)].set(low).at[tuple(beside)].set(largest)


def block_levels(rng, shape, cuts, low, high):
    def one(axis_at, parts):
        steps = jax.random.uniform(jax.random.fold_in(jax.random.fold_in(rng, 6), axis_at), (parts,), jnp.float32, low / len(cuts), high / len(cuts))
        return jnp.repeat(jnp.exp(steps), shape[axis_at] // parts).reshape((-1,) + (1,) * (len(shape) - axis_at - 1))

    level = one(*cuts[0])
    for cut in cuts[1:]:
        level = level * one(*cut)
    return level


def gaussian(own_key, dims, width, most, cuts=(), held_as=jnp.bfloat16):
    array = width * jax.random.normal(own_key, dims, jnp.float32)
    if cuts:
        array = array * block_levels(own_key, dims, cuts, -0.22, 0.18)
    return jnp.clip(array, -most, most).astype(held_as)


def setup_inputs(seed: int = 0) -> dict:
    splits = jax.random.split(jax.random.key(seed), 13)
    feats = gaussian(splits[0], (NODES, W), 1.0, 6.0, ((0, 32),))
    cotangent = gaussian(splits[1], (NODES, W), 1.0, 6.0, ((0, 32),))
    tile_table = draw_tile_table(jax.random.fold_in(splits[12], 71), 0)
    edge_src = touch_ends(jax.random.randint(splits[3], (DEV_COUNT, EB), 0, BLK_SLAB), jax.random.fold_in(splits[3], 1), 0, BLK_SLAB - 1).astype(jnp.int32)
    edge_tile = touch_ends(jax.random.randint(splits[4], (DEV_COUNT, EB), 0, TILE_DEV), jax.random.fold_in(splits[4], 1), 0, TILE_DEV - 1).astype(jnp.int32)
    edge_slot = touch_ends(jax.random.randint(splits[5], (DEV_COUNT, EB), 0, SLOTS), jax.random.fold_in(splits[5], 1), 0, SLOTS - 1).astype(jnp.int32)
    edge_count = draw_edge_count(jax.random.fold_in(splits[12], 71), 0)
    slot_block = touch_ends(jax.random.randint(splits[7], (N_SLAB, SLOTS), 0, BLK_SLAB), jax.random.fold_in(splits[7], 1), 0, BLK_SLAB - 1).astype(jnp.int32)
    norm_gain = jnp.clip(1.0 + 0.18 * jax.random.normal(splits[8], (2 * W,), jnp.float32), 0.1, 1.9)
    w_in = gaussian(splits[9], (2 * W, HID), (2 * W) ** -0.5, 0.375)
    b_in = gaussian(splits[10], (HID,), 0.5, 3.0, (), jnp.float32)
    w_out = gaussian(splits[11], (HID, W), HID ** -0.5, 0.25)
    return {"feats": feats, "cotangent": cotangent, "tile_table": tile_table, "edge_src": edge_src, "edge_tile": edge_tile, "edge_slot": edge_slot, "edge_count": edge_count, "slot_block": slot_block, "norm_gain": norm_gain, "w_in": w_in, "b_in": b_in, "w_out": w_out}


RMS_EPS = 1e-06
EXACT_MODE = lax.Precision.HIGHEST

def node_forward(feat_rows, agg_rows, norm_gain, w_in, b_in, w_out):
    wide_in = jnp.concatenate([feat_rows.astype(jnp.float32), agg_rows], axis=1)
    inv_rms = lax.rsqrt(lax.optimization_barrier(jnp.mean(wide_in * wide_in, axis=1, keepdims=True)) + RMS_EPS)
    normed = (wide_in * inv_rms * norm_gain).astype(jnp.bfloat16)
    pre_act = jnp.dot(normed, w_in, preferred_element_type=jnp.float32) + b_in
    activated = jax.nn.silu(pre_act).astype(jnp.bfloat16)
    updated = (feat_rows.astype(jnp.float32) + jnp.dot(activated, w_out, preferred_element_type=jnp.float32)).astype(jnp.bfloat16)
    return (wide_in, inv_rms, normed, pre_act, activated, updated)

def node_backward(cot_rows, wide_in, inv_rms, normed, pre_act, activated, norm_gain, w_in, w_out):
    d_act = lax.dot_general(cot_rows, w_out, (((1,), (1,)), ((), ())), preferred_element_type=jnp.float32)
    sigmoid_pre = jax.nn.sigmoid(pre_act)
    d_pre = d_act * sigmoid_pre * (1.0 + pre_act * (1.0 - sigmoid_pre))
    d_pre_b = d_pre.astype(jnp.bfloat16)
    d_normed = lax.dot_general(d_pre_b, w_in, (((1,), (1,)), ((), ())), preferred_element_type=jnp.float32)
    d_scaled = d_normed * norm_gain
    inner_mean = lax.optimization_barrier(jnp.mean(d_scaled * wide_in, axis=1, keepdims=True))
    d_wide = inv_rms * d_scaled - inv_rms * inv_rms * inv_rms * wide_in * inner_mean
    grad_terms = (lax.optimization_barrier(jnp.sum(d_normed * wide_in * inv_rms, axis=0)), lax.dot_general(normed, d_pre_b, (((0,), (0,)), ((), ())), preferred_element_type=jnp.float32), lax.optimization_barrier(jnp.sum(d_pre, axis=0)), lax.dot_general(activated, cot_rows, (((0,), (0,)), ((), ())), preferred_element_type=jnp.float32))
    return (d_wide, grad_terms)

def reference(feats, cotangent, tile_table, edge_src, edge_tile, edge_slot, edge_count, slot_block, norm_gain, w_in, b_in, w_out):
    device_total = N_SLAB * N_REP
    block_total = N_SLAB * BLK_SLAB
    rows_dev = BLK_DEV * B
    slab_feats = feats.reshape(N_SLAB, BLK_SLAB, B, W)
    tile_sets = tile_table.reshape(device_total, TILE_DEV, B, B)
    slot_ids = jnp.arange(SLOTS, dtype=jnp.int32)
    slab_ids = jnp.arange(N_SLAB, dtype=jnp.int32)
    dest_slab = (slab_ids[:, None] + (slot_ids // SLOT_CAP)[None, :] - NEIGH // 2) % N_SLAB
    targets = (dest_slab * BLK_SLAB + slot_block).astype(jnp.int32)
    positions = jnp.arange(EB, dtype=jnp.int32)
    device_ids = jnp.arange(device_total, dtype=jnp.int32)

    def forward_device(aggregate, device):
        slab_no = device // N_REP
        is_live = positions < edge_count[device]
        sources = slab_feats[slab_no][edge_src[device]].astype(jnp.float32)
        tiles_now = tile_sets[device][edge_tile[device]].astype(jnp.float32)
        messages = jnp.einsum('eij,ejc->eic', tiles_now, sources, precision=EXACT_MODE)
        segment = jnp.where(is_live, edge_slot[device], SLOTS).astype(jnp.int32)
        partial_sums = jax.ops.segment_sum(messages, segment, num_segments=SLOTS + 1)[:SLOTS]
        return (aggregate.at[targets[slab_no]].add(partial_sums), None)
    aggregate = lax.scan(forward_device, jnp.zeros((block_total, B, W), jnp.float32), device_ids)[0]
    feat_dev = feats.reshape(device_total, rows_dev, W)
    cot_dev = cotangent.reshape(device_total, rows_dev, W)
    agg_dev = aggregate.reshape(device_total, rows_dev, W)

    def node_device(pieces):
        feat_rows, agg_rows, cot_rows = pieces
        wide_in, inv_rms, normed, pre_act, activated, updated = node_forward(feat_rows, agg_rows, norm_gain, w_in, b_in, w_out)
        d_wide, grad_terms = node_backward(cot_rows, wide_in, inv_rms, normed, pre_act, activated, norm_gain, w_in, w_out)
        return (updated, d_wide, grad_terms)
    updated, d_wide, grad_terms = lax.map(node_device, (feat_dev, agg_dev, cot_dev))
    scale = NODES ** (-0.5)
    grads = [lax.optimization_barrier(jnp.sum(term, axis=0)) * scale for term in grad_terms]
    d_agg = d_wide[:, :, W:].astype(jnp.bfloat16).reshape(block_total, B, W)

    def backward_device(from_edges, device):
        slab_no = device // N_REP
        is_live = positions < edge_count[device]
        slot_grads = d_agg[targets[slab_no]]
        grads_now = slot_grads[edge_slot[device]].astype(jnp.float32)
        tiles_now = tile_sets[device][edge_tile[device]].astype(jnp.float32)
        contrib = jnp.einsum('eji,ejc->eic', tiles_now, grads_now, precision=EXACT_MODE)
        segment = jnp.where(is_live, edge_src[device], BLK_SLAB).astype(jnp.int32)
        per_block = jax.ops.segment_sum(contrib, segment, num_segments=BLK_SLAB + 1)[:BLK_SLAB]
        return (from_edges.at[slab_no].add(per_block), None)
    from_edges = lax.scan(backward_device, jnp.zeros((N_SLAB, BLK_SLAB, B, W), jnp.float32), device_ids)[0]
    grad_feats = cotangent.astype(jnp.float32) + d_wide[:, :, :W].reshape(NODES, W) + from_edges.reshape(NODES, W)
    return (updated.reshape(NODES, W), grad_feats, grads[0], grads[1], grads[2], grads[3])
```

```python
import functools
import math

import jax
import jax.numpy as jnp
from jax import lax
from jax.experimental import pallas as pl
from jax.experimental.pallas import tpu as pltpu
from jax.sharding import PartitionSpec as P

NEIGH = 8
SLOT_CAP = 8
MID = NEIGH // 2

RMS_EPS = 1e-06
EDGE_UNROLL = 32
PIECES = 4
LANES = 128
VMEM = pl.BlockSpec(memory_space=pltpu.VMEM)
SMEM = pl.BlockSpec(memory_space=pltpu.SMEM)
ANY = pl.BlockSpec(memory_space=pl.ANY)
DMA = pltpu.SemaphoreType.DMA
FAR_FIRST = sorted((g for g in range(NEIGH) if g != MID), key=lambda g: -abs(g - MID))
ORDER = FAR_FIRST + [MID]
SHARE_ORDER = [MID] + FAR_FIRST
PREV_F, LAST_F, PREV_B, LAST_B, PREV_A, LAST_A = range(6)
f32, bf16, i32 = jnp.float32, jnp.bfloat16, jnp.int32


def place():
    slab, rep = lax.axis_index("slab"), lax.axis_index("rep")
    core = lax.rem(rep, 2)
    return slab, rep, core, lax.div(rep, 2), rep + 1 - 2 * core


def slab_at(offset):
    n_slab = lax.axis_size("slab")
    return lax.rem(lax.axis_index("slab") + offset + n_slab, n_slab)


class Wires:
    def __init__(self, send_sems, recv_sems):
        self.send_sems, self.recv_sems = send_sems, recv_sems
        self.used = 0
        self.sending = []

    def send(self, src, dst, slab, rep):
        copy = pltpu.make_async_remote_copy(
            src_ref=src,
            dst_ref=dst,
            send_sem=self.send_sems.at[self.used],
            recv_sem=self.recv_sems.at[self.used],
            device_id=(slab, rep),
            device_id_type=pl.DeviceIdType.MESH,
        )
        self.used += 1
        copy.start()
        self.sending.append(copy)
        return copy

    def flush(self):
        for copy in self.sending:
            copy.wait_send()
        self.sending = []


def peers_of(halves):
    _, _, core, half, _ = place()
    to = [lax.rem(half + d, halves) * 2 + core for d in range(1, halves)]
    origin = [lax.rem(half + halves - d, halves) * 2 + core for d in range(1, halves)]
    return to, origin


def greet(halves, n_slab):
    slab, rep, _, _, partner = place()
    to, _ = peers_of(halves)
    targets = [(slab, partner)] + [(slab, peer) for peer in to]
    targets += [(slab_at(d), rep) for d in range(1, n_slab)]
    barrier = pltpu.get_barrier_semaphore()
    for target in targets:
        pl.semaphore_signal(barrier, inc=1, device_id=target, device_id_type=pl.DeviceIdType.MESH)
    return lambda: pl.semaphore_wait(barrier, len(targets))


def column(row):
    return jnp.broadcast_to(row, (LANES, row.shape[1])).T


def link_entries(row, live):
    n = row.shape[1]
    keys = column(row)
    at = lax.broadcasted_iota(i32, (n, LANES), 0)
    lane = lax.broadcasted_iota(i32, (n, LANES), 1)
    prev = []
    for p in range(n // LANES):
        same = (keys == row[:, p * LANES : (p + 1) * LANES]) & (at < lane + p * LANES)
        prev.append(jnp.max(jnp.where(same, at + 1, 0), axis=0, keepdims=True))
    last = jnp.max(jnp.where((keys == lane) & (at < live), at + 1, 0), axis=0, keepdims=True)
    return jnp.concatenate(prev, axis=1), last


def turn_of(slot):
    g = slot // SLOT_CAP
    pos = jnp.zeros_like(slot)
    for p, which in enumerate(SHARE_ORDER):
        pos = jnp.where(g == which, p, pos)
    return pos * SLOT_CAP + (slot - g * SLOT_CAP)


def link_arrivals(slot_block, first_block):
    slots = NEIGH * SLOT_CAP
    lane = lax.broadcasted_iota(i32, (1, slots), 1)
    row = jnp.zeros((1, slots), i32)
    for g in range(NEIGH):
        mine = slot_block[pl.ds(slab_at(MID - g), 1), :]
        row = jnp.where(lane // SLOT_CAP == g, mine, row)
    row = jnp.concatenate([row, jnp.full((1, LANES - slots), -1, i32)], axis=1)
    keys = column(row)
    order_c = turn_of(lax.broadcasted_iota(i32, (LANES, LANES), 0))
    order_r = turn_of(lax.broadcasted_iota(i32, (LANES, LANES), 1))
    lane = lax.broadcasted_iota(i32, (LANES, LANES), 1)
    same = (keys == row) & (order_c < order_r)
    prev = jnp.max(jnp.where(same, order_c + 1, 0), axis=0, keepdims=True)
    last = jnp.max(jnp.where(keys == lane + first_block, order_c + 1, 0), axis=0, keepdims=True)
    return prev, last


def run_edges(n, product, prev, hist):
    unroll = math.gcd(n, EDGE_UNROLL)

    def turn(i, carry):
        work = [product(i * unroll + u) for u in range(unroll)]
        for u, term in enumerate(work):
            e = i * unroll + u
            hist[e + 1] = hist[prev(e)] + term
        return carry

    lax.fori_loop(0, n // unroll, turn, 0)


def share(wires, halves, arrived, ready, done, idle):
    slab, _, core, half, partner = place()
    to, _ = peers_of(halves)
    across, on, onward = {}, {}, {}

    def pass_on(g):
        onward[g] = []
        for d in range(1, halves):
            across[g][d - 1].wait_recv()
            theirs = arrived.at[g, core, lax.rem(half + halves - d, halves)]
            onward[g].append(wires.send(theirs, theirs, slab, partner))

    def finish(g):
        for copy in [on[g]] + onward[g]:
            copy.wait_recv()
        done(g)

    lag, late = 2, 4
    for i in range(NEIGH + late):
        if i < NEIGH:
            g = SHARE_ORDER[i]
            ready(g)
            own = arrived.at[g, core, half]
            across[g] = [wires.send(own, own, slab, peer) for peer in to]
            on[g] = wires.send(own, own, slab, partner)
            if i == NEIGH - 1:
                idle()
        if lag <= i < NEIGH + lag:
            pass_on(SHARE_ORDER[i - lag])
        if i >= late:
            finish(SHARE_ORDER[i - late])


def layer_kernel(
    halves,
    n_slab,
    each,
    own,
    cot,
    table_hbm,
    src_v,
    slot_v,
    srcs,
    tiles,
    slots,
    count,
    slot_block_v,
    slot_block,
    gain,
    w_in,
    b_in,
    w_out,
    updated,
    grad_feats,
    grads,
    table,
    slab_feats,
    meta_v,
    meta,
    hist,
    part,
    from_core,
    to_far,
    from_far,
    outgoing,
    arrived,
    agg_hist,
    normed_s,
    act_s,
    d_pre_s,
    d_own,
    gathered,
    out_b,
    arrived_b,
    packed,
    w_core,
    w_to,
    w_far,
    w_rep,
    w_pieces,
    w_piece,
    e_part,
    e_core,
    e_to,
    e_far,
    local_sems,
    send_sems,
    recv_sems,
):
    slab, rep, core, half, partner = place()
    to, origin = peers_of(halves)
    wires = Wires(send_sems, recv_sems)
    nb, rows_b, width = own.shape
    n_rep = 2 * halves
    per_rep = SLOT_CAP // n_rep
    entries = srcs.shape[1]
    peers = range(1, n_slab)

    load = pltpu.make_async_copy(table_hbm, table, local_sems.at[0])
    load.start()
    arrive = greet(halves, n_slab)

    meta_v[...] = jnp.zeros_like(meta_v)
    prev, last = link_entries(slot_v[...], count[0])
    meta_v[PREV_F : PREV_F + 1, :] = prev
    meta_v[LAST_F : LAST_F + 1, 0:LANES] = last
    prev, last = link_entries(src_v[...], count[0])
    meta_v[PREV_B : PREV_B + 1, :] = prev
    meta_v[LAST_B : LAST_B + 1, 0:LANES] = last
    prev, last = link_arrivals(slot_block_v, rep * nb)
    meta_v[PREV_A : PREV_A + 1, 0:LANES] = prev
    meta_v[LAST_A : LAST_A + 1, 0:LANES] = last
    known = pltpu.make_async_copy(meta_v, meta, local_sems.at[1])
    known.start()
    hist[0] = jnp.zeros((rows_b, width), f32)
    agg_hist[0] = jnp.zeros((rows_b, width), f32)
    arrive()

    def blocks(ref, who, at, n):
        return ref.at[pl.ds(who * nb + at, n)]

    def gather_begin(mine, out, at, n):
        src = mine.at[pl.ds(at, n)]
        far = [wires.send(src, blocks(out, rep, at, n), slab, peer) for peer in to]
        near = wires.send(src, blocks(out, rep, at, n), slab, partner)
        return far, near

    def gather_forward(begun, out, at, n):
        onward = [begun[1]]
        for copy, who in zip(begun[0], origin):
            copy.wait_recv()
            ref = blocks(out, who, at, n)
            onward.append(wires.send(ref, ref, slab, partner))
        return onward

    step = nb // PIECES if nb % PIECES == 0 else nb
    starts = list(range(0, nb, step))
    begun = [gather_begin(own, slab_feats, at, step) for at in starts]
    slab_feats[pl.ds(rep * nb, nb)] = own[...]
    known.wait()
    load.wait()
    onward = []
    for at, b in zip(starts, begun):
        onward += gather_forward(b, slab_feats, at, step)
    for copy in onward:
        copy.wait_recv()

    run_edges(
        entries,
        lambda e: jnp.dot(table[tiles[0, e]], slab_feats[srcs[0, e]], preferred_element_type=f32),
        lambda e: meta[PREV_F, e],
        hist,
    )

    def slot_sum(g, c, h, j):
        slot = g * SLOT_CAP + (c * halves + h) * per_rep + j
        return hist[meta[LAST_F, slot]]

    first, cross, second = {}, {}, {}
    for g in ORDER:
        for h in range(halves):
            for j in range(per_rep):
                part[g, h, j] = slot_sum(g, 1 - core, h, j).astype(bf16)
        first[g] = wires.send(part.at[g], from_core.at[g], slab, partner)
    for g in ORDER:
        first[g].wait_recv()
        cross[g] = []
        for d in range(1, halves):
            h = lax.rem(half + d, halves)
            for j in range(per_rep):
                total = slot_sum(g, core, h, j) + from_core[g, h, j].astype(f32)
                to_far[d - 1, g, j] = total.astype(bf16)
            cross[g].append(
                wires.send(to_far.at[d - 1, g], from_far.at[d - 1, g], slab, h * 2 + core)
            )
    for g in ORDER:
        for copy in cross[g]:
            copy.wait_recv()
        for j in range(per_rep):
            total = slot_sum(g, core, half, j) + from_core[g, half, j].astype(f32)
            for d in range(1, halves):
                total = total + from_far[d - 1, g, j].astype(f32)
            if g == MID:
                arrived[g, core, half, j] = total.astype(bf16)
            else:
                outgoing[g, j] = total.astype(bf16)
        if g != MID:
            second[g] = wires.send(outgoing.at[g], arrived.at[g, core, half], slab_at(g - MID), rep)

    def ready(g):
        if g in second:
            second[g].wait_recv()

    def add_arrivals(g):
        for k in range(SLOT_CAP):
            c, h, j = k // (halves * per_rep), k // per_rep % halves, k % per_rep
            at = SHARE_ORDER.index(g) * SLOT_CAP + k
            agg_hist[at + 1] = agg_hist[meta[PREV_A, g * SLOT_CAP + k]] + arrived[g, c, h, j].astype(f32)

    share(wires, halves, arrived, ready, add_arrivals, lambda: None)

    rows = step * rows_b
    g_gain = jnp.zeros((1, 2 * width), f32)
    g_b = jnp.zeros((1, w_in.shape[1]), f32)
    begun = []
    for b0 in starts:
        at = pl.ds(b0 * rows_b, rows)
        feat = own[pl.ds(b0, step)].reshape(rows, width).astype(f32)
        cots = cot[at]
        agg = jnp.concatenate([agg_hist[meta[LAST_A, b0 + b]] for b in range(step)], axis=0)
        wide = jnp.concatenate([feat, agg], axis=1)
        inv = lax.rsqrt(jnp.mean(wide * wide, axis=1, keepdims=True) + RMS_EPS)
        scaled = wide * inv
        normed = (scaled * gain[...]).astype(bf16)
        pre = jnp.dot(normed, w_in[...], preferred_element_type=f32) + b_in[...]
        sg = jax.nn.sigmoid(pre)
        act = (pre * sg).astype(bf16)
        d_act = lax.dot_general(cots, w_out[...], (((1,), (1,)), ((), ())), preferred_element_type=f32)
        d_pre = d_act * sg * (1.0 + pre * (1.0 - sg))
        d_pre_b = d_pre.astype(bf16)
        d_normed = lax.dot_general(
            d_pre_b, w_in[...], (((1,), (1,)), ((), ())), preferred_element_type=f32
        )
        d_scaled = d_normed * gain[...]
        inner = jnp.mean(d_scaled * wide, axis=1, keepdims=True)
        d_wide = inv * d_scaled - inv * inv * inv * wide * inner
        for b in range(step):
            d_own[b0 + b] = d_wide[b * rows_b : (b + 1) * rows_b, width:].T.astype(bf16)
        begun.append(gather_begin(d_own, gathered, b0, step))
        grad_feats[at] = cots.astype(f32) + d_wide[:, :width]
        normed_s[at] = normed
        act_s[at] = act
        d_pre_s[at] = d_pre_b
        g_gain = g_gain + jnp.sum(d_normed * scaled, axis=0, keepdims=True)
        g_b = g_b + jnp.sum(d_pre, axis=0, keepdims=True)
        updated[at] = (feat + jnp.dot(act, w_out[...], preferred_element_type=f32)).astype(bf16)
    gathered[pl.ds(rep * nb, nb)] = d_own[...]

    over_rows = (((0,), (0,)), ((), ()))
    n_in, hidden = w_in.shape
    panels = hidden // width

    def weights_in(c):
        panel = lax.dot_general(
            normed_s[...], d_pre_s[:, width * c : width * (c + 1)], over_rows, preferred_element_type=f32
        )
        packed[n_in * c : n_in * (c + 1)] = panel.astype(bf16)

    onward = []
    for at, b in zip(starts[:-1], begun[:-1]):
        onward += gather_forward(b, gathered, at, step)
    n = n_in * panels
    g_out = lax.dot_general(act_s[...], cot[...], over_rows, preferred_element_type=f32)
    packed[n : n + hidden] = g_out.astype(bf16)
    n += hidden
    rest = [
        value[:, width * c : width * (c + 1)]
        for value in (g_gain, g_b)
        for c in range(value.shape[1] // width)
    ]
    rest.append(jnp.zeros((16 - len(rest), width), f32))
    packed[n : n + 16] = jnp.concatenate(rest, axis=0).astype(bf16)
    n += 16
    if packed.shape[0] > n:
        packed[n:] = jnp.zeros((packed.shape[0] - n, width), bf16)
    onward += gather_forward(begun[-1], gathered, starts[-1], step)
    for c in range(panels):
        weights_in(c)
    for copy in onward:
        copy.wait_recv()

    def pick(g, j):
        dest = slot_block[slab_at(MID - g), g * SLOT_CAP + (core * halves + half) * per_rep + j]
        return gathered[dest]

    second_b = {}
    for g in ORDER:
        for j in range(per_rep):
            if g == MID:
                arrived_b[g, core, half, j] = pick(g, j)
            else:
                out_b[g, j] = pick(g, j)
        if g != MID:
            second_b[g] = wires.send(
                out_b.at[g], arrived_b.at[g, core, half], slab_at(MID - g), rep
            )

    chunk = n_slab * each

    def of_rep(ref, h, c):
        return ref.at[pl.ds((h * 2 + c) * chunk, chunk)]

    near = []
    for d in list(range(1, halves)) + [0]:
        h = lax.rem(half + d, halves)
        near.append((d, h, wires.send(of_rep(packed, h, 1 - core), w_core.at[h], slab, partner)))
    w_cross = []
    for d, h, copy in near:
        copy.wait_recv()
        if d > 0:
            total = of_rep(packed, h, core)[...].astype(f32) + w_core[h].astype(f32)
            w_to[d - 1] = total.astype(bf16)
            w_cross.append(wires.send(w_to.at[d - 1], w_far.at[d - 1], slab, h * 2 + core))

    def ready_b(g):
        if g in second_b:
            second_b[g].wait_recv()

    w_slab = []

    def scatter_weights():
        total = of_rep(packed, half, core)[...].astype(f32) + w_core[half].astype(f32)
        for d, copy in enumerate(w_cross):
            copy.wait_recv()
            total = total + w_far[d].astype(f32)
        w_rep[...] = total.astype(bf16)
        for d in peers:
            peer = slab_at(d)
            w_slab.append(
                wires.send(w_rep.at[pl.ds(peer * each, each)], w_pieces.at[d - 1], peer, rep)
            )

    share(wires, halves, arrived_b, ready_b, lambda g: None, scatter_weights)

    total = w_rep[pl.ds(slab * each, each)].astype(f32)
    for d, copy in enumerate(w_slab):
        copy.wait_recv()
        total = total + w_pieces[d].astype(f32)
    w_piece[...] = total.astype(bf16)
    mine = grads.at[rep, pl.ds(slab * each, each)]
    mine[...] = w_piece[...]
    w_back = [wires.send(w_piece, mine, slab_at(d), rep) for d in peers]

    def product_b(e):
        slot = slots[0, e]
        k = lax.rem(slot, SLOT_CAP)
        given = arrived_b[
            lax.div(slot, SLOT_CAP),
            lax.div(k, halves * per_rep),
            lax.rem(lax.div(k, per_rep), halves),
            lax.rem(k, per_rep),
        ]
        return jnp.dot(given, table[tiles[0, e]], preferred_element_type=f32)

    run_edges(entries, product_b, lambda e: meta[PREV_B, e], hist)

    def block_sum(h, c, b):
        return hist[meta[LAST_B, (h * 2 + c) * nb + b]]

    folds = {}
    for d in list(range(1, halves)) + [0]:
        h = lax.rem(half + d, halves)
        for b0 in starts:
            for b in range(b0, b0 + step):
                e_part[d, b] = block_sum(h, 1 - core, b).astype(bf16)
            at = pl.ds(b0, step)
            folds[d, b0] = wires.send(e_part.at[d, at], e_core.at[d, at], slab, partner)
    far = {}
    for d in range(1, halves):
        h = lax.rem(half + d, halves)
        for b0 in starts:
            folds[d, b0].wait_recv()
            for b in range(b0, b0 + step):
                e_to[d - 1, b] = (block_sum(h, core, b) + e_core[d, b].astype(f32)).astype(bf16)
            at = pl.ds(b0, step)
            far[d, b0] = wires.send(e_to.at[d - 1, at], e_far.at[d - 1, at], slab, h * 2 + core)
    for copy in w_back:
        copy.wait_recv()
    w_far_g = [wires.send(grads.at[rep], grads.at[rep], slab, peer) for peer in to]
    w_on = [wires.send(grads.at[rep], grads.at[rep], slab, partner)]
    for b0 in starts:
        folds[0, b0].wait_recv()
        for d in range(1, halves):
            far[d, b0].wait_recv()
        for b in range(b0, b0 + step):
            total = block_sum(half, core, b) + e_core[0, b].astype(f32)
            for d in range(1, halves):
                total = total + e_far[d - 1, b].astype(f32)
            at = pl.ds(b * rows_b, rows_b)
            grad_feats[at] = grad_feats[at] + total.T
    for copy, who in zip(w_far_g, origin):
        copy.wait_recv()
        w_on.append(wires.send(grads.at[who], grads.at[who], slab, partner))
    for copy in w_on:
        copy.wait_recv()
    wires.flush()


def final_kernel(scale, updated_in, feats_in, grads, updated, grad_feats, g_gain, g_in, g_b, g_out, sems):
    moves = [
        pltpu.make_async_copy(updated_in, updated, sems.at[0]),
        pltpu.make_async_copy(feats_in, grad_feats, sems.at[1]),
    ]
    for move in moves:
        move.start()
    width = grads.shape[1]

    def part(at, n):
        return grads[at : at + n].astype(f32) * scale

    n, panels = g_in.shape[0], g_in.shape[1] // width
    for c in range(panels):
        g_in[:, width * c : width * (c + 1)] = part(n * c, n)
    n = n * panels
    g_out[...] = part(n, g_out.shape[0])
    rest = part(n + g_out.shape[0], 16)
    at = 0
    for ref in (g_gain, g_b):
        for c in range(ref.shape[1] // width):
            ref[:, width * c : width * (c + 1)] = rest[at : at + 1]
            at += 1
    for move in moves:
        move.wait()


def body(
    feats,
    cotangent,
    tile_table,
    edge_src,
    edge_tile,
    edge_slot,
    edge_count,
    slot_block,
    norm_gain,
    w_in,
    b_in,
    w_out,
):
    n_slab = lax.axis_size("slab")
    n_rep = lax.axis_size("rep")
    halves = n_rep // 2
    rows_dev, width = feats.shape
    hidden = w_out.shape[0]
    rows_b = tile_table.shape[1]
    nb = rows_dev // rows_b
    slab_blocks = nb * n_rep
    entries = edge_src.shape[1]
    per_rep = SLOT_CAP // n_rep
    used = w_in.size // width + hidden + 16
    each = -(-used // (n_slab * n_rep * 16)) * 16
    chunk = n_slab * each
    shape = jax.ShapeDtypeStruct
    n_sems = 224 + 2 * n_slab

    def block(*lead, dtype=bf16):
        return pltpu.VMEM((*lead, rows_b, width), dtype)

    def weights(*lead):
        return pltpu.VMEM((*lead, width), bf16)

    updated, grad_feats, grads = pl.pallas_call(
        functools.partial(layer_kernel, halves, n_slab, each),
        out_shape=(
            shape((rows_dev, width), bf16),
            shape((rows_dev, width), f32),
            shape((n_rep, chunk, width), bf16),
        ),
        in_specs=[VMEM, VMEM, ANY, VMEM, VMEM] + [SMEM] * 4 + [VMEM, SMEM] + [VMEM] * 4,
        out_specs=(VMEM,) * 3,
        scratch_shapes=[
            pltpu.VMEM(tile_table.shape, bf16),
            block(slab_blocks),
            pltpu.VMEM((8, entries), i32),
            pltpu.SMEM((8, entries), i32),
            block(entries + 1, dtype=f32),
            block(NEIGH, halves, per_rep),
            block(NEIGH, halves, per_rep),
            block(halves - 1, NEIGH, per_rep),
            block(halves - 1, NEIGH, per_rep),
            block(NEIGH, per_rep),
            block(NEIGH, 2, halves, per_rep),
            block(NEIGH * SLOT_CAP + 1, dtype=f32),
            pltpu.VMEM((rows_dev, 2 * width), bf16),
            pltpu.VMEM((rows_dev, hidden), bf16),
            pltpu.VMEM((rows_dev, hidden), bf16),
            block(nb),
            block(slab_blocks),
            block(NEIGH, per_rep),
            block(NEIGH, 2, halves, per_rep),
            weights(n_rep * chunk),
            weights(halves, chunk),
            weights(halves - 1, chunk),
            weights(halves - 1, chunk),
            weights(chunk),
            weights(n_slab - 1, each),
            weights(each),
            block(halves, nb),
            block(halves, nb),
            block(halves - 1, nb),
            block(halves - 1, nb),
            DMA((2,)),
            DMA((n_sems,)),
            DMA((n_sems,)),
        ],
        compiler_params=pltpu.CompilerParams(
            collective_id=0, has_side_effects=True, vmem_limit_bytes=58 << 20
        ),
    )(
        feats.reshape(nb, rows_b, width),
        cotangent,
        tile_table,
        edge_src,
        edge_slot,
        edge_src,
        edge_tile,
        edge_slot,
        edge_count,
        slot_block,
        slot_block,
        norm_gain.reshape(1, -1),
        w_in,
        b_in.reshape(1, -1),
        w_out,
    )
    scale = float(rows_dev * n_slab * n_rep) ** (-0.5)
    updated, grad_feats, grad_gain, grad_w_in, grad_b_in, grad_w_out = pl.pallas_call(
        functools.partial(final_kernel, scale),
        out_shape=(
            shape((rows_dev, width), bf16),
            shape((rows_dev, width), f32),
            shape((1, 2 * width), f32),
            shape(w_in.shape, f32),
            shape((1, hidden), f32),
            shape(w_out.shape, f32),
        ),
        in_specs=[ANY, ANY, VMEM],
        out_specs=(ANY, ANY) + (VMEM,) * 4,
        scratch_shapes=[DMA((2,))],
    )(updated, grad_feats, grads.reshape(-1, width))
    return (
        updated,
        grad_feats,
        grad_gain.reshape(-1),
        grad_w_in,
        grad_b_in.reshape(-1),
        grad_w_out,
    )


def solution(mesh):
    rows = P(("slab", "rep"), None)
    placed = (rows, rows, P(("slab", "rep"), None, None)) + (rows,) * 3 + (P(("slab", "rep")),) + (P(),) * 5
    return jax.shard_map(
        body,
        mesh=mesh,
        in_specs=placed,
        out_specs=(rows, rows, P(), P(), P(), P()),
        check_vma=False,
    )
```

```python
import functools
import math

import jax
import jax.numpy as jnp
from jax import lax
from jax.experimental import pallas as pl
from jax.experimental.pallas import tpu as pltpu
from jax.sharding import PartitionSpec as P

NEIGH = 8
SLOT_CAP = 8
MID = NEIGH // 2

RMS_EPS = 1e-06
EDGE_UNROLL = 32
PIECES = 4
LANES = 128
VMEM = pl.BlockSpec(memory_space=pltpu.VMEM)
SMEM = pl.BlockSpec(memory_space=pltpu.SMEM)
ANY = pl.BlockSpec(memory_space=pl.ANY)
DMA = pltpu.SemaphoreType.DMA
FAR_FIRST = sorted((g for g in range(NEIGH) if g != MID), key=lambda g: -abs(g - MID))
ORDER = FAR_FIRST + [MID]
SHARE_ORDER = [MID] + FAR_FIRST
PREV_F, LAST_F, PREV_B, LAST_B, PREV_A, LAST_A = range(6)
f32, bf16, i32 = jnp.float32, jnp.bfloat16, jnp.int32


def place():
    slab, rep = lax.axis_index("slab"), lax.axis_index("rep")
    core = lax.rem(rep, 2)
    return slab, rep, core, lax.div(rep, 2), rep + 1 - 2 * core


def slab_at(offset):
    n_slab = lax.axis_size("slab")
    return lax.rem(lax.axis_index("slab") + offset + n_slab, n_slab)


class Wires:
    def __init__(self, send_sems, recv_sems):
        self.send_sems, self.recv_sems = send_sems, recv_sems
        self.used = 0
        self.sending = []

    def send(self, src, dst, slab, rep):
        copy = pltpu.make_async_remote_copy(
            src_ref=src,
            dst_ref=dst,
            send_sem=self.send_sems.at[self.used],
            recv_sem=self.recv_sems.at[self.used],
            device_id=(slab, rep),
            device_id_type=pl.DeviceIdType.MESH,
        )
        self.used += 1
        copy.start()
        self.sending.append(copy)
        return copy

    def flush(self):
        for copy in self.sending:
            copy.wait_send()
        self.sending = []


def peers_of(halves):
    _, _, core, half, _ = place()
    to = [lax.rem(half + d, halves) * 2 + core for d in range(1, halves)]
    origin = [lax.rem(half + halves - d, halves) * 2 + core for d in range(1, halves)]
    return to, origin


def greet(halves, n_slab):
    slab, rep, _, _, partner = place()
    to, _ = peers_of(halves)
    targets = [(slab, partner)] + [(slab, peer) for peer in to]
    targets += [(slab_at(d), rep) for d in range(1, n_slab)]
    barrier = pltpu.get_barrier_semaphore()
    for target in targets:
        pl.semaphore_signal(barrier, inc=1, device_id=target, device_id_type=pl.DeviceIdType.MESH)
    return lambda: pl.semaphore_wait(barrier, len(targets))


def column(row):
    return jnp.broadcast_to(row, (LANES, row.shape[1])).T


def link_entries(row, live):
    n = row.shape[1]
    keys = column(row)
    at = lax.broadcasted_iota(i32, (n, LANES), 0)
    lane = lax.broadcasted_iota(i32, (n, LANES), 1)
    prev = []
    for p in range(n // LANES):
        same = (keys == row[:, p * LANES : (p + 1) * LANES]) & (at < lane + p * LANES)
        prev.append(jnp.max(jnp.where(same, at + 1, 0), axis=0, keepdims=True))
    last = jnp.max(jnp.where((keys == lane) & (at < live), at + 1, 0), axis=0, keepdims=True)
    return jnp.concatenate(prev, axis=1), last


def turn_of(slot):
    g = slot // SLOT_CAP
    pos = jnp.zeros_like(slot)
    for p, which in enumerate(SHARE_ORDER):
        pos = jnp.where(g == which, p, pos)
    return pos * SLOT_CAP + (slot - g * SLOT_CAP)


def link_arrivals(slot_block, first_block):
    slots = NEIGH * SLOT_CAP
    lane = lax.broadcasted_iota(i32, (1, slots), 1)
    row = jnp.zeros((1, slots), i32)
    for g in range(NEIGH):
        mine = slot_block[pl.ds(slab_at(MID - g), 1), :]
        row = jnp.where(lane // SLOT_CAP == g, mine, row)
    row = jnp.concatenate([row, jnp.full((1, LANES - slots), -1, i32)], axis=1)
    keys = column(row)
    order_c = turn_of(lax.broadcasted_iota(i32, (LANES, LANES), 0))
    order_r = turn_of(lax.broadcasted_iota(i32, (LANES, LANES), 1))
    lane = lax.broadcasted_iota(i32, (LANES, LANES), 1)
    same = (keys == row) & (order_c < order_r)
    prev = jnp.max(jnp.where(same, order_c + 1, 0), axis=0, keepdims=True)
    last = jnp.max(jnp.where(keys == lane + first_block, order_c + 1, 0), axis=0, keepdims=True)
    return prev, last


def run_edges(n, product, prev, hist):
    unroll = math.gcd(n, EDGE_UNROLL)

    def turn(i, carry):
        work = [product(i * unroll + u) for u in range(unroll)]
        for u, term in enumerate(work):
            e = i * unroll + u
            hist[e + 1] = hist[prev(e)] + term
        return carry

    lax.fori_loop(0, n // unroll, turn, 0)


def share(wires, halves, arrived, ready, done, idle):
    slab, _, core, half, partner = place()
    to, _ = peers_of(halves)
    across, on, onward = {}, {}, {}

    def pass_on(g):
        onward[g] = []
        for d in range(1, halves):
            across[g][d - 1].wait_recv()
            theirs = arrived.at[g, core, lax.rem(half + halves - d, halves)]
            onward[g].append(wires.send(theirs, theirs, slab, partner))

    def finish(g):
        for copy in [on[g]] + onward[g]:
            copy.wait_recv()
        done(g)

    lag, late = 2, 4
    for i in range(NEIGH + late):
        if i < NEIGH:
            g = SHARE_ORDER[i]
            ready(g)
            own = arrived.at[g, core, half]
            across[g] = [wires.send(own, own, slab, peer) for peer in to]
            on[g] = wires.send(own, own, slab, partner)
            if i == NEIGH - 1:
                idle()
        if lag <= i < NEIGH + lag:
            pass_on(SHARE_ORDER[i - lag])
        if i >= late:
            finish(SHARE_ORDER[i - late])


def layer_kernel(
    halves,
    n_slab,
    each,
    own,
    cot,
    table_hbm,
    src_v,
    slot_v,
    srcs,
    tiles,
    slots,
    count,
    slot_block_v,
    slot_block,
    gain,
    w_in,
    b_in,
    w_out,
    updated,
    grad_feats,
    grads,
    table,
    slab_feats,
    meta_v,
    meta,
    hist,
    part,
    from_core,
    to_far,
    from_far,
    outgoing,
    arrived,
    agg_hist,
    normed_s,
    act_s,
    d_pre_s,
    d_own,
    gathered,
    out_b,
    arrived_b,
    packed,
    w_core,
    w_to,
    w_far,
    w_rep,
    w_pieces,
    w_piece,
    e_part,
    e_core,
    e_to,
    e_far,
    local_sems,
    send_sems,
    recv_sems,
):
    slab, rep, core, half, partner = place()
    to, origin = peers_of(halves)
    wires = Wires(send_sems, recv_sems)
    nb, rows_b, width = own.shape
    n_rep = 2 * halves
    per_rep = SLOT_CAP // n_rep
    entries = srcs.shape[1]
    peers = range(1, n_slab)

    load = pltpu.make_async_copy(table_hbm, table, local_sems.at[0])
    load.start()
    arrive = greet(halves, n_slab)

    meta_v[...] = jnp.zeros_like(meta_v)
    prev, last = link_entries(slot_v[...], count[0])
    meta_v[PREV_F : PREV_F + 1, :] = prev
    meta_v[LAST_F : LAST_F + 1, 0:LANES] = last
    prev, last = link_entries(src_v[...], count[0])
    meta_v[PREV_B : PREV_B + 1, :] = prev
    meta_v[LAST_B : LAST_B + 1, 0:LANES] = last
    prev, last = link_arrivals(slot_block_v, rep * nb)
    meta_v[PREV_A : PREV_A + 1, 0:LANES] = prev
    meta_v[LAST_A : LAST_A + 1, 0:LANES] = last
    known = pltpu.make_async_copy(meta_v, meta, local_sems.at[1])
    known.start()
    hist[0] = jnp.zeros((rows_b, width), f32)
    agg_hist[0] = jnp.zeros((rows_b, width), f32)
    arrive()

    def blocks(ref, who, at, n):
        return ref.at[pl.ds(who * nb + at, n)]

    def gather_begin(mine, out, at, n):
        src = mine.at[pl.ds(at, n)]
        far = [wires.send(src, blocks(out, rep, at, n), slab, peer) for peer in to]
        near = wires.send(src, blocks(out, rep, at, n), slab, partner)
        return far, near

    def gather_forward(begun, out, at, n):
        onward = [begun[1]]
        for copy, who in zip(begun[0], origin):
            copy.wait_recv()
            ref = blocks(out, who, at, n)
            onward.append(wires.send(ref, ref, slab, partner))
        return onward

    step = nb // PIECES if nb % PIECES == 0 else nb
    starts = list(range(0, nb, step))
    begun = [gather_begin(own, slab_feats, at, step) for at in starts]
    slab_feats[pl.ds(rep * nb, nb)] = own[...]
    known.wait()
    load.wait()
    onward = []
    for at, b in zip(starts, begun):
        onward += gather_forward(b, slab_feats, at, step)
    for copy in onward:
        copy.wait_recv()

    run_edges(
        entries,
        lambda e: jnp.dot(table[tiles[0, e]], slab_feats[srcs[0, e]], preferred_element_type=f32),
        lambda e: meta[PREV_F, e],
        hist,
    )

    def slot_sum(g, c, h, j):
        slot = g * SLOT_CAP + (c * halves + h) * per_rep + j
        return hist[meta[LAST_F, slot]]

    first, cross, second = {}, {}, {}
    for g in ORDER:
        for h in range(halves):
            for j in range(per_rep):
                part[g, h, j] = slot_sum(g, 1 - core, h, j).astype(bf16)
        first[g] = wires.send(part.at[g], from_core.at[g], slab, partner)
    for g in ORDER:
        first[g].wait_recv()
        cross[g] = []
        for d in range(1, halves):
            h = lax.rem(half + d, halves)
            for j in range(per_rep):
                total = slot_sum(g, core, h, j) + from_core[g, h, j].astype(f32)
                to_far[d - 1, g, j] = total.astype(bf16)
            cross[g].append(
                wires.send(to_far.at[d - 1, g], from_far.at[d - 1, g], slab, h * 2 + core)
            )
    for g in ORDER:
        for copy in cross[g]:
            copy.wait_recv()
        for j in range(per_rep):
            total = slot_sum(g, core, half, j) + from_core[g, half, j].astype(f32)
            for d in range(1, halves):
                total = total + from_far[d - 1, g, j].astype(f32)
            if g == MID:
                arrived[g, core, half, j] = total.astype(bf16)
            else:
                outgoing[g, j] = total.astype(bf16)
        if g != MID:
            second[g] = wires.send(outgoing.at[g], arrived.at[g, core, half], slab_at(g - MID), rep)

    def ready(g):
        if g in second:
            second[g].wait_recv()

    def add_arrivals(g):
        for k in range(SLOT_CAP):
            c, h, j = k // (halves * per_rep), k // per_rep % halves, k % per_rep
            at = SHARE_ORDER.index(g) * SLOT_CAP + k
            agg_hist[at + 1] = agg_hist[meta[PREV_A, g * SLOT_CAP + k]] + arrived[g, c, h, j].astype(f32)

    share(wires, halves, arrived, ready, add_arrivals, lambda: None)

    rows = step * rows_b
    g_gain = jnp.zeros((1, 2 * width), f32)
    g_b = jnp.zeros((1, w_in.shape[1]), f32)
    begun = []
    for b0 in starts:
        at = pl.ds(b0 * rows_b, rows)
        feat = own[pl.ds(b0, step)].reshape(rows, width).astype(f32)
        cots = cot[at]
        agg = jnp.concatenate([agg_hist[meta[LAST_A, b0 + b]] for b in range(step)], axis=0)
        wide = jnp.concatenate([feat, agg], axis=1)
        inv = lax.rsqrt(jnp.mean(wide * wide, axis=1, keepdims=True) + RMS_EPS)
        scaled = wide * inv
        normed = (scaled * gain[...]).astype(bf16)
        pre = jnp.dot(normed, w_in[...], preferred_element_type=f32) + b_in[...]
        sg = jax.nn.sigmoid(pre)
        act = (pre * sg).astype(bf16)
        d_act = lax.dot_general(cots, w_out[...], (((1,), (1,)), ((), ())), preferred_element_type=f32)
        d_pre = d_act * sg * (1.0 + pre * (1.0 - sg))
        d_pre_b = d_pre.astype(bf16)
        d_normed = lax.dot_general(
            d_pre_b, w_in[...], (((1,), (1,)), ((), ())), preferred_element_type=f32
        )
        d_scaled = d_normed * gain[...]
        inner = jnp.mean(d_scaled * wide, axis=1, keepdims=True)
        d_wide = inv * d_scaled - inv * inv * inv * wide * inner
        for b in range(step):
            d_own[b0 + b] = d_wide[b * rows_b : (b + 1) * rows_b, width:].T.astype(bf16)
        begun.append(gather_begin(d_own, gathered, b0, step))
        grad_feats[at] = cots.astype(f32) + d_wide[:, :width]
        normed_s[at] = normed
        act_s[at] = act
        d_pre_s[at] = d_pre_b
        g_gain = g_gain + jnp.sum(d_normed * scaled, axis=0, keepdims=True)
        g_b = g_b + jnp.sum(d_pre, axis=0, keepdims=True)
        updated[at] = (feat + jnp.dot(act, w_out[...], preferred_element_type=f32)).astype(bf16)
    gathered[pl.ds(rep * nb, nb)] = d_own[...]

    over_rows = (((0,), (0,)), ((), ()))
    n_in, hidden = w_in.shape
    panels = hidden // width

    def weights_in(c):
        panel = lax.dot_general(
            normed_s[...], d_pre_s[:, width * c : width * (c + 1)], over_rows, preferred_element_type=f32
        )
        packed[n_in * c : n_in * (c + 1)] = panel.astype(bf16)

    onward = []
    for at, b in zip(starts[:-1], begun[:-1]):
        onward += gather_forward(b, gathered, at, step)
    n = n_in * panels
    g_out = lax.dot_general(act_s[...], cot[...], over_rows, preferred_element_type=f32)
    packed[n : n + hidden] = g_out.astype(bf16)
    n += hidden
    rest = [
        value[:, width * c : width * (c + 1)]
        for value in (g_gain, g_b)
        for c in range(value.shape[1] // width)
    ]
    rest.append(jnp.zeros((16 - len(rest), width), f32))
    packed[n : n + 16] = jnp.concatenate(rest, axis=0).astype(bf16)
    n += 16
    if packed.shape[0] > n:
        packed[n:] = jnp.zeros((packed.shape[0] - n, width), bf16)
    onward += gather_forward(begun[-1], gathered, starts[-1], step)
    for c in range(panels):
        weights_in(c)
    for copy in onward:
        copy.wait_recv()

    def pick(g, j):
        dest = slot_block[slab_at(MID - g), g * SLOT_CAP + (core * halves + half) * per_rep + j]
        return gathered[dest]

    second_b = {}
    for g in ORDER:
        for j in range(per_rep):
            if g == MID:
                arrived_b[g, core, half, j] = pick(g, j)
            else:
                out_b[g, j] = pick(g, j)
        if g != MID:
            second_b[g] = wires.send(
                out_b.at[g], arrived_b.at[g, core, half], slab_at(MID - g), rep
            )

    chunk = n_slab * each

    def of_rep(ref, h, c):
        return ref.at[pl.ds((h * 2 + c) * chunk, chunk)]

    near = []
    for d in list(range(1, halves)) + [0]:
        h = lax.rem(half + d, halves)
        near.append((d, h, wires.send(of_rep(packed, h, 1 - core), w_core.at[h], slab, partner)))
    w_cross = []
    for d, h, copy in near:
        copy.wait_recv()
        if d > 0:
            total = of_rep(packed, h, core)[...].astype(f32) + w_core[h].astype(f32)
            w_to[d - 1] = total.astype(bf16)
            w_cross.append(wires.send(w_to.at[d - 1], w_far.at[d - 1], slab, h * 2 + core))

    def ready_b(g):
        if g in second_b:
            second_b[g].wait_recv()

    w_slab = []

    def scatter_weights():
        total = of_rep(packed, half, core)[...].astype(f32) + w_core[half].astype(f32)
        for d, copy in enumerate(w_cross):
            copy.wait_recv()
            total = total + w_far[d].astype(f32)
        w_rep[...] = total.astype(bf16)
        for d in peers:
            peer = slab_at(d)
            w_slab.append(
                wires.send(w_rep.at[pl.ds(peer * each, each)], w_pieces.at[d - 1], peer, rep)
            )

    share(wires, halves, arrived_b, ready_b, lambda g: None, scatter_weights)

    total = w_rep[pl.ds(slab * each, each)].astype(f32)
    for d, copy in enumerate(w_slab):
        copy.wait_recv()
        total = total + w_pieces[d].astype(f32)
    w_piece[...] = total.astype(bf16)
    mine = grads.at[rep, pl.ds(slab * each, each)]
    mine[...] = w_piece[...]
    w_back = [wires.send(w_piece, mine, slab_at(d), rep) for d in peers]

    def product_b(e):
        slot = slots[0, e]
        k = lax.rem(slot, SLOT_CAP)
        given = arrived_b[
            lax.div(slot, SLOT_CAP),
            lax.div(k, halves * per_rep),
            lax.rem(lax.div(k, per_rep), halves),
            lax.rem(k, per_rep),
        ]
        return jnp.dot(given, table[tiles[0, e]], preferred_element_type=f32)

    run_edges(entries, product_b, lambda e: meta[PREV_B, e], hist)

    def block_sum(h, c, b):
        return hist[meta[LAST_B, (h * 2 + c) * nb + b]]

    folds = {}
    for d in list(range(1, halves)) + [0]:
        h = lax.rem(half + d, halves)
        for b0 in starts:
            for b in range(b0, b0 + step):
                e_part[d, b] = block_sum(h, 1 - core, b).astype(bf16)
            at = pl.ds(b0, step)
            folds[d, b0] = wires.send(e_part.at[d, at], e_core.at[d, at], slab, partner)
    far = {}
    for d in range(1, halves):
        h = lax.rem(half + d, halves)
        for b0 in starts:
            folds[d, b0].wait_recv()
            for b in range(b0, b0 + step):
                e_to[d - 1, b] = (block_sum(h, core, b) + e_core[d, b].astype(f32)).astype(bf16)
            at = pl.ds(b0, step)
            far[d, b0] = wires.send(e_to.at[d - 1, at], e_far.at[d - 1, at], slab, h * 2 + core)
    for copy in w_back:
        copy.wait_recv()
    w_far_g = [wires.send(grads.at[rep], grads.at[rep], slab, peer) for peer in to]
    w_on = [wires.send(grads.at[rep], grads.at[rep], slab, partner)]
    for b0 in starts:
        folds[0, b0].wait_recv()
        for d in range(1, halves):
            far[d, b0].wait_recv()
        for b in range(b0, b0 + step):
            total = block_sum(half, core, b) + e_core[0, b].astype(f32)
            for d in range(1, halves):
                total = total + e_far[d - 1, b].astype(f32)
            at = pl.ds(b * rows_b, rows_b)
            grad_feats[at] = grad_feats[at] + total.T
    for copy, who in zip(w_far_g, origin):
        copy.wait_recv()
        w_on.append(wires.send(grads.at[who], grads.at[who], slab, partner))
    for copy in w_on:
        copy.wait_recv()
    wires.flush()


def final_kernel(scale, updated_in, feats_in, grads, updated, grad_feats, g_gain, g_in, g_b, g_out):
    updated[...] = updated_in[...]
    grad_feats[...] = feats_in[...]
    width = grads.shape[1]

    def part(at, n):
        return grads[at : at + n].astype(f32) * scale

    n, panels = g_in.shape[0], g_in.shape[1] // width
    for c in range(panels):
        g_in[:, width * c : width * (c + 1)] = part(n * c, n)
    n = n * panels
    g_out[...] = part(n, g_out.shape[0])
    rest = part(n + g_out.shape[0], 16)
    at = 0
    for ref in (g_gain, g_b):
        for c in range(ref.shape[1] // width):
            ref[:, width * c : width * (c + 1)] = rest[at : at + 1]
            at += 1


def body(
    feats,
    cotangent,
    tile_table,
    edge_src,
    edge_tile,
    edge_slot,
    edge_count,
    slot_block,
    norm_gain,
    w_in,
    b_in,
    w_out,
):
    n_slab = lax.axis_size("slab")
    n_rep = lax.axis_size("rep")
    halves = n_rep // 2
    rows_dev, width = feats.shape
    hidden = w_out.shape[0]
    rows_b = tile_table.shape[1]
    nb = rows_dev // rows_b
    slab_blocks = nb * n_rep
    entries = edge_src.shape[1]
    per_rep = SLOT_CAP // n_rep
    used = w_in.size // width + hidden + 16
    each = -(-used // (n_slab * n_rep * 16)) * 16
    chunk = n_slab * each
    shape = jax.ShapeDtypeStruct
    n_sems = 224 + 2 * n_slab

    def block(*lead, dtype=bf16):
        return pltpu.VMEM((*lead, rows_b, width), dtype)

    def weights(*lead):
        return pltpu.VMEM((*lead, width), bf16)

    updated, grad_feats, grads = pl.pallas_call(
        functools.partial(layer_kernel, halves, n_slab, each),
        out_shape=(
            shape((rows_dev, width), bf16),
            shape((rows_dev, width), f32),
            shape((n_rep, chunk, width), bf16),
        ),
        in_specs=[VMEM, VMEM, ANY, VMEM, VMEM] + [SMEM] * 4 + [VMEM, SMEM] + [VMEM] * 4,
        out_specs=(VMEM,) * 3,
        scratch_shapes=[
            pltpu.VMEM(tile_table.shape, bf16),
            block(slab_blocks),
            pltpu.VMEM((8, entries), i32),
            pltpu.SMEM((8, entries), i32),
            block(entries + 1, dtype=f32),
            block(NEIGH, halves, per_rep),
            block(NEIGH, halves, per_rep),
            block(halves - 1, NEIGH, per_rep),
            block(halves - 1, NEIGH, per_rep),
            block(NEIGH, per_rep),
            block(NEIGH, 2, halves, per_rep),
            block(NEIGH * SLOT_CAP + 1, dtype=f32),
            pltpu.VMEM((rows_dev, 2 * width), bf16),
            pltpu.VMEM((rows_dev, hidden), bf16),
            pltpu.VMEM((rows_dev, hidden), bf16),
            block(nb),
            block(slab_blocks),
            block(NEIGH, per_rep),
            block(NEIGH, 2, halves, per_rep),
            weights(n_rep * chunk),
            weights(halves, chunk),
            weights(halves - 1, chunk),
            weights(halves - 1, chunk),
            weights(chunk),
            weights(n_slab - 1, each),
            weights(each),
            block(halves, nb),
            block(halves, nb),
            block(halves - 1, nb),
            block(halves - 1, nb),
            DMA((2,)),
            DMA((n_sems,)),
            DMA((n_sems,)),
        ],
        compiler_params=pltpu.CompilerParams(
            collective_id=0, has_side_effects=True, vmem_limit_bytes=58 << 20
        ),
    )(
        feats.reshape(nb, rows_b, width),
        cotangent,
        tile_table,
        edge_src,
        edge_slot,
        edge_src,
        edge_tile,
        edge_slot,
        edge_count,
        slot_block,
        slot_block,
        norm_gain.reshape(1, -1),
        w_in,
        b_in.reshape(1, -1),
        w_out,
    )
    scale = float(rows_dev * n_slab * n_rep) ** (-0.5)
    updated, grad_feats, grad_gain, grad_w_in, grad_b_in, grad_w_out = pl.pallas_call(
        functools.partial(final_kernel, scale),
        out_shape=(
            shape((rows_dev, width), bf16),
            shape((rows_dev, width), f32),
            shape((1, 2 * width), f32),
            shape(w_in.shape, f32),
            shape((1, hidden), f32),
            shape(w_out.shape, f32),
        ),
        in_specs=[VMEM] * 3,
        out_specs=(VMEM,) * 6,
    )(updated, grad_feats, grads.reshape(-1, width))
    return (
        updated,
        grad_feats,
        grad_gain.reshape(-1),
        grad_w_in,
        grad_b_in.reshape(-1),
        grad_w_out,
    )


def solution(mesh):
    rows = P(("slab", "rep"), None)
    placed = (rows, rows, P(("slab", "rep"), None, None)) + (rows,) * 3 + (P(("slab", "rep")),) + (P(),) * 5
    return jax.shard_map(
        body,
        mesh=mesh,
        in_specs=placed,
        out_specs=(rows, rows, P(), P(), P(), P()),
        check_vma=False,
    )
```

```python
import functools
import math

import jax
import jax.numpy as jnp
from jax import lax
from jax.experimental import pallas as pl
from jax.experimental.pallas import tpu as pltpu
from jax.sharding import PartitionSpec as P

NEIGH = 8
SLOT_CAP = 8
MID = NEIGH // 2

RMS_EPS = 1e-06
EDGE_UNROLL = 64
PIECES = 4
LANES = 128
VMEM = pl.BlockSpec(memory_space=pltpu.VMEM)
SMEM = pl.BlockSpec(memory_space=pltpu.SMEM)
ANY = pl.BlockSpec(memory_space=pl.ANY)
DMA = pltpu.SemaphoreType.DMA
DIRECT = [MID - 1, MID + 1]
FOLDED = sorted((g for g in range(NEIGH) if g != MID and g not in DIRECT), key=lambda g: abs(g - MID))
AWAY = DIRECT + FOLDED
TURNS = [MID] + AWAY
DIRECT_B = []
FOLDED_B = [g for g in sorted(range(NEIGH), key=lambda g: abs(g - MID)) if g != MID and g not in DIRECT_B]
LAG = 3
PREV_F, LAST_F, PREV_B, LAST_B, PREV_A, LAST_A = range(6)
f32, bf16, i32 = jnp.float32, jnp.bfloat16, jnp.int32


def place():
    slab, rep = lax.axis_index("slab"), lax.axis_index("rep")
    core = lax.rem(rep, 2)
    return slab, rep, core, lax.div(rep, 2), rep + 1 - 2 * core


def slab_at(offset):
    n_slab = lax.axis_size("slab")
    return lax.rem(lax.axis_index("slab") + offset + n_slab, n_slab)


class Wires:
    def __init__(self, send_sems, recv_sems):
        self.send_sems, self.recv_sems = send_sems, recv_sems
        self.used = 0
        self.sending = []

    def send(self, src, dst, slab, rep):
        copy = pltpu.make_async_remote_copy(
            src_ref=src,
            dst_ref=dst,
            send_sem=self.send_sems.at[self.used],
            recv_sem=self.recv_sems.at[self.used],
            device_id=(slab, rep),
            device_id_type=pl.DeviceIdType.MESH,
        )
        self.used += 1
        copy.start()
        self.sending.append(copy)
        return copy

    def flush(self):
        for copy in self.sending:
            copy.wait_send()
        self.sending = []


def peers_of(halves):
    _, _, core, half, _ = place()
    to = [lax.rem(half + d, halves) * 2 + core for d in range(1, halves)]
    origin = [lax.rem(half + halves - d, halves) * 2 + core for d in range(1, halves)]
    return to, origin


def greet(halves, n_slab):
    slab, rep, _, _, partner = place()
    to, _ = peers_of(halves)
    targets = [(slab, partner)] + [(slab, peer) for peer in to]
    targets += [(slab_at(d), rep) for d in range(1, n_slab)]
    barrier = pltpu.get_barrier_semaphore()
    for target in targets:
        pl.semaphore_signal(barrier, inc=1, device_id=target, device_id_type=pl.DeviceIdType.MESH)
    return lambda: pl.semaphore_wait(barrier, len(targets))


def column(row):
    return jnp.broadcast_to(row, (LANES, row.shape[1])).T


def link_entries(row, live):
    n = row.shape[1]
    keys = column(row)
    at = lax.broadcasted_iota(i32, (n, LANES), 0)
    lane = lax.broadcasted_iota(i32, (n, LANES), 1)
    prev = []
    for p in range(n // LANES):
        same = (keys == row[:, p * LANES : (p + 1) * LANES]) & (at < lane + p * LANES)
        prev.append(jnp.max(jnp.where(same, at + 1, 0), axis=0, keepdims=True))
    last = jnp.max(jnp.where((keys == lane) & (at < live), at + 1, 0), axis=0, keepdims=True)
    return jnp.concatenate(prev, axis=1), last


def turn_of(slot):
    g = slot // SLOT_CAP
    pos = jnp.zeros_like(slot)
    for p, which in enumerate(TURNS):
        pos = jnp.where(g == which, p, pos)
    return pos * SLOT_CAP + (slot - g * SLOT_CAP)


def link_arrivals(slot_block, halves):
    _, _, core, half, _ = place()
    slots = NEIGH * SLOT_CAP
    per_core, per_rep = SLOT_CAP // 2, SLOT_CAP // (2 * halves)
    lane = lax.broadcasted_iota(i32, (1, slots), 1)
    row = jnp.zeros((1, slots), i32)
    for g in range(NEIGH):
        mine = slot_block[pl.ds(slab_at(MID - g), 1), :]
        row = jnp.where(lane // SLOT_CAP == g, mine, row)
    row = jnp.concatenate([row, jnp.full((1, LANES - slots), -1, i32)], axis=1)
    keys = column(row)
    slot = lax.broadcasted_iota(i32, (LANES, LANES), 0)
    lane = lax.broadcasted_iota(i32, (LANES, LANES), 1)
    g, k = slot // SLOT_CAP, slot % SLOT_CAP
    of_core = k // per_core == core
    of_rep = of_core & (k % per_core // per_rep == half)
    held = of_rep | (g == MID)
    for d in DIRECT:
        held = held | (of_core & (g == d))
    order_c, order_r = turn_of(slot), turn_of(lane)
    prev = jnp.max(
        jnp.where((keys == row) & held & (order_c < order_r), order_c + 1, 0), axis=0, keepdims=True
    )
    last = jnp.max(jnp.where((keys == lane) & held, order_c + 1, 0), axis=0, keepdims=True)
    return prev, last


def run_edges(n, product, prev, hist):
    unroll = math.gcd(n, EDGE_UNROLL)

    def turn(i, carry):
        work = [product(i * unroll + u) for u in range(unroll)]
        for u, term in enumerate(work):
            e = i * unroll + u
            hist[e + 1] = hist[prev(e)] + term
        return carry

    lax.fori_loop(0, n // unroll, turn, 0)


def share(wires, halves, arrived, ready, idle):
    slab, _, core, half, partner = place()
    to, _ = peers_of(halves)
    across, on = {}, []

    def pass_on(g):
        for d in range(1, halves):
            across[g][d - 1].wait_recv()
            theirs = arrived.at[g, core, lax.rem(half + halves - d, halves)]
            on.append(wires.send(theirs, theirs, slab, partner))

    for g in DIRECT_B:
        ready(g)
        on.append(wires.send(arrived.at[g, core], arrived.at[g, core], slab, partner))
    for i in range(len(FOLDED_B) + LAG):
        if i < len(FOLDED_B):
            g = FOLDED_B[i]
            ready(g)
            own = arrived.at[g, core, half]
            across[g] = [wires.send(own, own, slab, peer) for peer in to]
            on.append(wires.send(own, own, slab, partner))
            if i == len(FOLDED_B) - 1:
                idle()
        if i >= LAG:
            pass_on(FOLDED_B[i - LAG])
    for copy in on:
        copy.wait_recv()


def fold(wires, halves, starts, step, block_sum, bufs, between, finish):
    slab, _, core, half, partner = place()
    part, from_core, to_far, from_far = bufs
    near, far = {}, {}
    for d in list(range(1, halves)) + [0]:
        h = lax.rem(half + d, halves)
        for b0 in starts:
            for b in range(b0, b0 + step):
                part[d, b] = block_sum(h, 1 - core, b).astype(bf16)
            at = pl.ds(b0, step)
            near[d, b0] = wires.send(part.at[d, at], from_core.at[d, at], slab, partner)
    for d in range(1, halves):
        h = lax.rem(half + d, halves)
        for b0 in starts:
            near[d, b0].wait_recv()
            for b in range(b0, b0 + step):
                to_far[d - 1, b] = (block_sum(h, core, b) + from_core[d, b].astype(f32)).astype(bf16)
            at = pl.ds(b0, step)
            far[d, b0] = wires.send(to_far.at[d - 1, at], from_far.at[d - 1, at], slab, h * 2 + core)
    between()
    for b0 in starts:
        near[0, b0].wait_recv()
        for d in range(1, halves):
            far[d, b0].wait_recv()
        totals = []
        for b in range(b0, b0 + step):
            total = block_sum(half, core, b) + from_core[0, b].astype(f32)
            for d in range(1, halves):
                total = total + from_far[d - 1, b].astype(f32)
            totals.append(total)
        finish(b0, totals)


def layer_kernel(
    halves,
    n_slab,
    each,
    feats_hbm,
    cot_hbm,
    table_hbm,
    srcs_hbm,
    tiles_hbm,
    slots_hbm,
    count_hbm,
    slot_block_hbm,
    gain_hbm,
    w_in_hbm,
    b_in_hbm,
    w_out_hbm,
    updated_hbm,
    grad_feats_hbm,
    grads_hbm,
    cot,
    src_v,
    slot_v,
    srcs,
    tiles,
    slots,
    count,
    slot_block_v,
    slot_block,
    gain,
    w_in,
    b_in,
    w_out,
    updated,
    grad_feats,
    grads,
    table,
    slab_feats,
    meta_v,
    meta,
    hist,
    part,
    from_core,
    to_far,
    from_far,
    outgoing,
    arrived,
    agg_hist,
    a_part,
    a_core,
    a_to,
    a_far,
    normed_s,
    act_s,
    d_pre_s,
    d_own,
    gathered,
    out_b,
    arrived_b,
    packed,
    w_core,
    w_to,
    w_far,
    w_rep,
    w_pieces,
    w_piece,
    e_part,
    e_core,
    e_to,
    e_far,
    local_sems,
    send_sems,
    recv_sems,
):
    slab, rep, core, half, partner = place()
    to, origin = peers_of(halves)
    wires = Wires(send_sems, recv_sems)
    nb, rows_b, width = d_own.shape
    n_rep = 2 * halves
    per_rep = SLOT_CAP // n_rep
    entries = srcs.shape[1]
    peers = range(1, n_slab)

    arrive = greet(halves, n_slab)
    own = slab_feats.at[pl.ds(rep * nb, nb)]
    loads = [
        pltpu.make_async_copy(src, dst, local_sems.at[i])
        for i, (src, dst) in enumerate(
            [
                (slots_hbm, slot_v),
                (srcs_hbm, src_v),
                (slot_block_hbm, slot_block_v),
                (count_hbm, count),
                (feats_hbm, own),
                (srcs_hbm, srcs),
                (tiles_hbm, tiles),
                (slots_hbm, slots),
                (slot_block_hbm, slot_block),
                (table_hbm, table),
                (cot_hbm, cot),
                (gain_hbm, gain),
                (w_in_hbm, w_in),
                (b_in_hbm, b_in),
                (w_out_hbm, w_out),
            ]
        )
    ]
    local_used = len(loads)
    for load in loads:
        load.start()
    for load in loads[:4]:
        load.wait()

    meta_v[...] = jnp.zeros_like(meta_v)
    prev, last = link_entries(slot_v[...], count[0])
    meta_v[PREV_F : PREV_F + 1, :] = prev
    meta_v[LAST_F : LAST_F + 1, 0:LANES] = last
    prev, last = link_entries(src_v[...], count[0])
    meta_v[PREV_B : PREV_B + 1, :] = prev
    meta_v[LAST_B : LAST_B + 1, 0:LANES] = last
    prev, last = link_arrivals(slot_block_v, halves)
    meta_v[PREV_A : PREV_A + 1, 0:LANES] = prev
    meta_v[LAST_A : LAST_A + 1, 0:LANES] = last
    known = pltpu.make_async_copy(meta_v, meta, local_sems.at[local_used])
    known.start()
    hist[0] = jnp.zeros((rows_b, width), f32)
    agg_hist[0] = jnp.zeros((rows_b, width), f32)
    arrive()
    loads[4].wait()

    def blocks(ref, who, at, n):
        return ref.at[pl.ds(who * nb + at, n)]

    def gather_begin(mine, out, at, n):
        src = mine.at[pl.ds(at, n)]
        far = [wires.send(src, blocks(out, rep, at, n), slab, peer) for peer in to]
        near = wires.send(src, blocks(out, rep, at, n), slab, partner)
        return far, near

    def gather_forward(begun, out, at, n):
        onward = [begun[1]]
        for copy, who in zip(begun[0], origin):
            copy.wait_recv()
            ref = blocks(out, who, at, n)
            onward.append(wires.send(ref, ref, slab, partner))
        return onward

    step = nb // PIECES if nb % PIECES == 0 else nb
    starts = list(range(0, nb, step))
    begun = [gather_begin(own, slab_feats, at, step) for at in starts]
    known.wait()
    for load in loads[5:]:
        load.wait()
    onward = []
    for at, b in zip(starts, begun):
        onward += gather_forward(b, slab_feats, at, step)
    for copy in onward:
        copy.wait_recv()

    run_edges(
        entries,
        lambda e: jnp.dot(table[tiles[0, e]], slab_feats[srcs[0, e]], preferred_element_type=f32),
        lambda e: meta[PREV_F, e],
        hist,
    )

    def slot_sum(g, c, h, j):
        slot = g * SLOT_CAP + (c * halves + h) * per_rep + j
        return hist[meta[LAST_F, slot]]

    first, cross, second = {}, {}, {}
    for g in AWAY:
        for h in range(halves):
            for j in range(per_rep):
                part[g, h, j] = slot_sum(g, 1 - core, h, j).astype(bf16)
        first[g] = wires.send(part.at[g], from_core.at[g], slab, partner)

    def core_sum(g, h, j):
        return slot_sum(g, core, h, j) + from_core[g, h, j].astype(f32)

    for g in DIRECT:
        first[g].wait_recv()
        for h in range(halves):
            for j in range(per_rep):
                outgoing[g, h, j] = core_sum(g, h, j).astype(bf16)
        second[g] = wires.send(outgoing.at[g], arrived.at[g], slab_at(g - MID), rep)
    for g in FOLDED:
        first[g].wait_recv()
        cross[g] = []
        for d in range(1, halves):
            h = lax.rem(half + d, halves)
            for j in range(per_rep):
                to_far[d - 1, g, j] = core_sum(g, h, j).astype(bf16)
            cross[g].append(
                wires.send(to_far.at[d - 1, g], from_far.at[d - 1, g], slab, h * 2 + core)
            )
    for g in FOLDED:
        for copy in cross[g]:
            copy.wait_recv()
        for j in range(per_rep):
            total = core_sum(g, half, j)
            for d in range(1, halves):
                total = total + from_far[d - 1, g, j].astype(f32)
            outgoing[g, 0, j] = total.astype(bf16)
        second[g] = wires.send(outgoing.at[g, 0], arrived.at[g, 0], slab_at(g - MID), rep)

    def add_to(g, c, h, j, value):
        k = (c * halves + h) * per_rep + j
        at = TURNS.index(g) * SLOT_CAP + k
        agg_hist[at + 1] = agg_hist[meta[PREV_A, g * SLOT_CAP + k]] + value

    for c in range(2):
        for h in range(halves):
            for j in range(per_rep):
                add_to(MID, c, h, j, slot_sum(MID, c, h, j))
    for g in DIRECT:
        second[g].wait_recv()
        for h in range(halves):
            for j in range(per_rep):
                add_to(g, core, h, j, arrived[g, h, j].astype(f32))
    for g in FOLDED:
        second[g].wait_recv()
        for j in range(per_rep):
            add_to(g, core, half, j, arrived[g, 0, j].astype(f32))

    rows = step * rows_b
    g_gains, g_bs, begun = [], [], []

    def update_nodes(b0, totals):
        at = pl.ds(b0 * rows_b, rows)
        feat = own[pl.ds(b0, step)].reshape(rows, width).astype(f32)
        cots = cot[at]
        agg = jnp.concatenate(totals, axis=0)
        wide = jnp.concatenate([feat, agg], axis=1)
        inv = lax.rsqrt(jnp.mean(wide * wide, axis=1, keepdims=True) + RMS_EPS)
        scaled = wide * inv
        normed = (scaled * gain[...]).astype(bf16)
        pre = jnp.dot(normed, w_in[...], preferred_element_type=f32) + b_in[...]
        sg = jax.nn.sigmoid(pre)
        act = (pre * sg).astype(bf16)
        d_act = lax.dot_general(cots, w_out[...], (((1,), (1,)), ((), ())), preferred_element_type=f32)
        d_pre = d_act * sg * (1.0 + pre * (1.0 - sg))
        d_pre_b = d_pre.astype(bf16)
        d_normed = lax.dot_general(
            d_pre_b, w_in[...], (((1,), (1,)), ((), ())), preferred_element_type=f32
        )
        d_scaled = d_normed * gain[...]
        inner = jnp.mean(d_scaled * wide, axis=1, keepdims=True)
        d_wide = inv * d_scaled - inv * inv * inv * wide * inner
        for b in range(step):
            d_own[b0 + b] = d_wide[b * rows_b : (b + 1) * rows_b, width:].T.astype(bf16)
        begun.append(gather_begin(d_own, gathered, b0, step))
        grad_feats[at] = cots.astype(f32) + d_wide[:, :width]
        normed_s[at] = normed
        act_s[at] = act
        d_pre_s[at] = d_pre_b
        g_gains.append(jnp.sum(d_normed * scaled, axis=0, keepdims=True))
        g_bs.append(jnp.sum(d_pre, axis=0, keepdims=True))
        updated[at] = (feat + jnp.dot(act, w_out[...], preferred_element_type=f32)).astype(bf16)

    fold(
        wires,
        halves,
        starts,
        step,
        lambda h, c, b: agg_hist[meta[LAST_A, (h * 2 + c) * nb + b]],
        (a_part, a_core, a_to, a_far),
        lambda: None,
        update_nodes,
    )
    g_gain, g_b = sum(g_gains), sum(g_bs)
    gathered[pl.ds(rep * nb, nb)] = d_own[...]
    stores = [pltpu.make_async_copy(updated, updated_hbm, local_sems.at[local_used + 1])]
    stores[0].start()

    over_rows = (((0,), (0,)), ((), ()))
    n_in, hidden = w_in.shape
    panels = hidden // width

    def weights_in(c):
        panel = lax.dot_general(
            normed_s[...], d_pre_s[:, width * c : width * (c + 1)], over_rows, preferred_element_type=f32
        )
        packed[n_in * c : n_in * (c + 1)] = panel.astype(bf16)

    onward = []
    for at, b in zip(starts[:-1], begun[:-1]):
        onward += gather_forward(b, gathered, at, step)
    n = n_in * panels
    g_out = lax.dot_general(act_s[...], cot[...], over_rows, preferred_element_type=f32)
    packed[n : n + hidden] = g_out.astype(bf16)
    n += hidden
    rest = [
        value[:, width * c : width * (c + 1)]
        for value in (g_gain, g_b)
        for c in range(value.shape[1] // width)
    ]
    rest.append(jnp.zeros((16 - len(rest), width), f32))
    packed[n : n + 16] = jnp.concatenate(rest, axis=0).astype(bf16)
    n += 16
    if packed.shape[0] > n:
        packed[n:] = jnp.zeros((packed.shape[0] - n, width), bf16)
    onward += gather_forward(begun[-1], gathered, starts[-1], step)
    for c in range(panels):
        weights_in(c)
    for copy in onward:
        copy.wait_recv()

    def pick(g, c, h, j):
        dest = slot_block[slab_at(MID - g), g * SLOT_CAP + (c * halves + h) * per_rep + j]
        return gathered[dest]

    second_b = {}
    for g in DIRECT_B:
        for h in range(halves):
            for j in range(per_rep):
                out_b[g, h, j] = pick(g, core, h, j)
        second_b[g] = wires.send(out_b.at[g], arrived_b.at[g, core], slab_at(MID - g), rep)
    for g in FOLDED_B:
        for j in range(per_rep):
            out_b[g, 0, j] = pick(g, core, half, j)
        second_b[g] = wires.send(out_b.at[g, 0], arrived_b.at[g, core, half], slab_at(MID - g), rep)
    for c in range(2):
        for h in range(halves):
            for j in range(per_rep):
                arrived_b[MID, c, h, j] = pick(MID, c, h, j)

    chunk = n_slab * each

    def of_rep(ref, h, c):
        return ref.at[pl.ds((h * 2 + c) * chunk, chunk)]

    near = []
    for d in list(range(1, halves)) + [0]:
        h = lax.rem(half + d, halves)
        near.append((d, h, wires.send(of_rep(packed, h, 1 - core), w_core.at[h], slab, partner)))
    w_cross = []
    for d, h, copy in near:
        copy.wait_recv()
        if d > 0:
            total = of_rep(packed, h, core)[...].astype(f32) + w_core[h].astype(f32)
            w_to[d - 1] = total.astype(bf16)
            w_cross.append(wires.send(w_to.at[d - 1], w_far.at[d - 1], slab, h * 2 + core))

    w_slab = []

    def scatter_weights():
        total = of_rep(packed, half, core)[...].astype(f32) + w_core[half].astype(f32)
        for d, copy in enumerate(w_cross):
            copy.wait_recv()
            total = total + w_far[d].astype(f32)
        w_rep[...] = total.astype(bf16)
        for d in peers:
            peer = slab_at(d)
            w_slab.append(
                wires.send(w_rep.at[pl.ds(peer * each, each)], w_pieces.at[d - 1], peer, rep)
            )

    share(wires, halves, arrived_b, lambda g: second_b[g].wait_recv(), scatter_weights)

    total = w_rep[pl.ds(slab * each, each)].astype(f32)
    for d, copy in enumerate(w_slab):
        copy.wait_recv()
        total = total + w_pieces[d].astype(f32)
    w_piece[...] = total.astype(bf16)
    mine = grads.at[rep, pl.ds(slab * each, each)]
    mine[...] = w_piece[...]
    w_back = [wires.send(w_piece, mine, slab_at(d), rep) for d in peers]

    wires.flush()

    def product_b(e):
        slot = slots[0, e]
        k = lax.rem(slot, SLOT_CAP)
        given = arrived_b[
            lax.div(slot, SLOT_CAP),
            lax.div(k, halves * per_rep),
            lax.rem(lax.div(k, per_rep), halves),
            lax.rem(k, per_rep),
        ]
        return jnp.dot(given, table[tiles[0, e]], preferred_element_type=f32)

    run_edges(entries, product_b, lambda e: meta[PREV_B, e], hist)

    def block_sum(h, c, b):
        return hist[meta[LAST_B, (h * 2 + c) * nb + b]]

    w_far_g, w_on = [], []

    def spread_weights():
        for copy in w_back:
            copy.wait_recv()
        w_far_g.extend(wires.send(grads.at[rep], grads.at[rep], slab, peer) for peer in to)
        w_on.append(wires.send(grads.at[rep], grads.at[rep], slab, partner))

    def add_folded(b0, totals):
        for b, total in enumerate(totals):
            at = pl.ds((b0 + b) * rows_b, rows_b)
            grad_feats[at] = grad_feats[at] + total.T
        at = pl.ds(b0 * rows_b, rows)
        store = pltpu.make_async_copy(
            grad_feats.at[at], grad_feats_hbm.at[at], local_sems.at[local_used + 3 + b0 // step]
        )
        store.start()
        stores.append(store)

    fold(
        wires, halves, starts, step, block_sum, (e_part, e_core, e_to, e_far), spread_weights, add_folded
    )
    for copy, who in zip(w_far_g, origin):
        copy.wait_recv()
        w_on.append(wires.send(grads.at[who], grads.at[who], slab, partner))
    for copy in w_on:
        copy.wait_recv()
    stores.append(pltpu.make_async_copy(grads, grads_hbm, local_sems.at[local_used + 2]))
    stores[-1].start()
    wires.flush()
    for store in stores:
        store.wait()


def final_kernel(scale, updated_in, feats_in, grads, updated, grad_feats, g_gain, g_in, g_b, g_out):
    updated[...] = updated_in[...]
    grad_feats[...] = feats_in[...]
    width = grads.shape[1]

    def part(at, n):
        return grads[at : at + n].astype(f32) * scale

    n, panels = g_in.shape[0], g_in.shape[1] // width
    for c in range(panels):
        g_in[:, width * c : width * (c + 1)] = part(n * c, n)
    n = n * panels
    g_out[...] = part(n, g_out.shape[0])
    rest = part(n + g_out.shape[0], 16)
    at = 0
    for ref in (g_gain, g_b):
        for c in range(ref.shape[1] // width):
            ref[:, width * c : width * (c + 1)] = rest[at : at + 1]
            at += 1


def body(
    feats,
    cotangent,
    tile_table,
    edge_src,
    edge_tile,
    edge_slot,
    edge_count,
    slot_block,
    norm_gain,
    w_in,
    b_in,
    w_out,
):
    n_slab = lax.axis_size("slab")
    n_rep = lax.axis_size("rep")
    halves = n_rep // 2
    rows_dev, width = feats.shape
    hidden = w_out.shape[0]
    rows_b = tile_table.shape[1]
    nb = rows_dev // rows_b
    slab_blocks = nb * n_rep
    entries = edge_src.shape[1]
    per_rep = SLOT_CAP // n_rep
    used = w_in.size // width + hidden + 16
    each = -(-used // (n_slab * n_rep * 16)) * 16
    chunk = n_slab * each
    shape = jax.ShapeDtypeStruct
    n_sems = 224 + 2 * n_slab

    def block(*lead, dtype=bf16):
        return pltpu.VMEM((*lead, rows_b, width), dtype)

    def weights(*lead):
        return pltpu.VMEM((*lead, width), bf16)

    updated, grad_feats, grads = pl.pallas_call(
        functools.partial(layer_kernel, halves, n_slab, each),
        out_shape=(
            shape((rows_dev, width), bf16),
            shape((rows_dev, width), f32),
            shape((n_rep, chunk, width), bf16),
        ),
        in_specs=[ANY] * 12,
        out_specs=(ANY,) * 3,
        scratch_shapes=[
            pltpu.VMEM((rows_dev, width), bf16),
            pltpu.VMEM(edge_src.shape, i32),
            pltpu.VMEM(edge_slot.shape, i32),
            pltpu.SMEM(edge_src.shape, i32),
            pltpu.SMEM(edge_tile.shape, i32),
            pltpu.SMEM(edge_slot.shape, i32),
            pltpu.SMEM(edge_count.shape, i32),
            pltpu.VMEM(slot_block.shape, i32),
            pltpu.SMEM(slot_block.shape, i32),
            pltpu.VMEM((1, 2 * width), f32),
            pltpu.VMEM(w_in.shape, bf16),
            pltpu.VMEM((1, hidden), f32),
            pltpu.VMEM(w_out.shape, bf16),
            pltpu.VMEM((rows_dev, width), bf16),
            pltpu.VMEM((rows_dev, width), f32),
            weights(n_rep, chunk),
            pltpu.VMEM(tile_table.shape, bf16),
            block(slab_blocks),
            pltpu.VMEM((8, entries), i32),
            pltpu.SMEM((8, entries), i32),
            block(entries + 1, dtype=f32),
            block(NEIGH, halves, per_rep),
            block(NEIGH, halves, per_rep),
            block(halves - 1, NEIGH, per_rep),
            block(halves - 1, NEIGH, per_rep),
            block(NEIGH, halves, per_rep),
            block(NEIGH, halves, per_rep),
            block(NEIGH * SLOT_CAP + 1, dtype=f32),
            block(halves, nb),
            block(halves, nb),
            block(halves - 1, nb),
            block(halves - 1, nb),
            pltpu.VMEM((rows_dev, 2 * width), bf16),
            pltpu.VMEM((rows_dev, hidden), bf16),
            pltpu.VMEM((rows_dev, hidden), bf16),
            block(nb),
            block(slab_blocks),
            block(NEIGH, halves, per_rep),
            block(NEIGH, 2, halves, per_rep),
            weights(n_rep * chunk),
            weights(halves, chunk),
            weights(halves - 1, chunk),
            weights(halves - 1, chunk),
            weights(chunk),
            weights(n_slab - 1, each),
            weights(each),
            block(halves, nb),
            block(halves, nb),
            block(halves - 1, nb),
            block(halves - 1, nb),
            DMA((24 + PIECES,)),
            DMA((n_sems,)),
            DMA((n_sems,)),
        ],
        compiler_params=pltpu.CompilerParams(
            collective_id=0, has_side_effects=True, vmem_limit_bytes=58 << 20
        ),
    )(
        feats.reshape(nb, rows_b, width),
        cotangent,
        tile_table,
        edge_src,
        edge_tile,
        edge_slot,
        edge_count,
        slot_block,
        norm_gain.reshape(1, -1),
        w_in,
        b_in.reshape(1, -1),
        w_out,
    )
    scale = float(rows_dev * n_slab * n_rep) ** (-0.5)
    updated, grad_feats, grad_gain, grad_w_in, grad_b_in, grad_w_out = pl.pallas_call(
        functools.partial(final_kernel, scale),
        out_shape=(
            shape((rows_dev, width), bf16),
            shape((rows_dev, width), f32),
            shape((1, 2 * width), f32),
            shape(w_in.shape, f32),
            shape((1, hidden), f32),
            shape(w_out.shape, f32),
        ),
        in_specs=[VMEM] * 3,
        out_specs=(VMEM,) * 6,
    )(updated, grad_feats, grads.reshape(-1, width))
    return (
        updated,
        grad_feats,
        grad_gain.reshape(-1),
        grad_w_in,
        grad_b_in.reshape(-1),
        grad_w_out,
    )


def solution(mesh):
    rows = P(("slab", "rep"), None)
    placed = (rows, rows, P(("slab", "rep"), None, None)) + (rows,) * 3 + (P(("slab", "rep")),) + (P(),) * 5
    return jax.shard_map(
        body,
        mesh=mesh,
        in_specs=placed,
        out_specs=(rows, rows, P(), P(), P(), P()),
        check_vma=False,
    )
```

```python
import functools
import math

import jax
import jax.numpy as jnp
from jax import lax
from jax.experimental import pallas as pl
from jax.experimental.pallas import tpu as pltpu
from jax.sharding import PartitionSpec as P

NEIGH = 8
SLOT_CAP = 8
MID = NEIGH // 2

RMS_EPS = 1e-06
EDGE_UNROLL = 64
PIECES = 4
LANES = 128
VMEM = pl.BlockSpec(memory_space=pltpu.VMEM)
SMEM = pl.BlockSpec(memory_space=pltpu.SMEM)
ANY = pl.BlockSpec(memory_space=pl.ANY)
DMA = pltpu.SemaphoreType.DMA
DIRECT = [MID - 1, MID + 1]
FOLDED = sorted((g for g in range(NEIGH) if g != MID and g not in DIRECT), key=lambda g: abs(g - MID))
AWAY = DIRECT + FOLDED
TURNS = [MID] + AWAY
DIRECT_B = []
FOLDED_B = [g for g in sorted(range(NEIGH), key=lambda g: abs(g - MID)) if g != MID and g not in DIRECT_B]
LAG = 3
SCATTER_AT, COLLECT_AT = 3, 8
PREV_F, LAST_F, PREV_B, LAST_B, PREV_A, LAST_A = range(6)
f32, bf16, i32 = jnp.float32, jnp.bfloat16, jnp.int32


def place():
    slab, rep = lax.axis_index("slab"), lax.axis_index("rep")
    core = lax.rem(rep, 2)
    return slab, rep, core, lax.div(rep, 2), rep + 1 - 2 * core


def slab_at(offset):
    n_slab = lax.axis_size("slab")
    return lax.rem(lax.axis_index("slab") + offset + n_slab, n_slab)


class Wires:
    def __init__(self, send_sems, recv_sems):
        self.send_sems, self.recv_sems = send_sems, recv_sems
        self.used = 0
        self.sending = []

    def send(self, src, dst, slab, rep):
        copy = pltpu.make_async_remote_copy(
            src_ref=src,
            dst_ref=dst,
            send_sem=self.send_sems.at[self.used],
            recv_sem=self.recv_sems.at[self.used],
            device_id=(slab, rep),
            device_id_type=pl.DeviceIdType.MESH,
        )
        self.used += 1
        copy.start()
        self.sending.append(copy)
        return copy

    def flush(self, n=None):
        n = len(self.sending) if n is None else n
        for copy in self.sending[:n]:
            copy.wait_send()
        self.sending = self.sending[n:]


def peers_of(halves):
    _, _, core, half, _ = place()
    to = [lax.rem(half + d, halves) * 2 + core for d in range(1, halves)]
    origin = [lax.rem(half + halves - d, halves) * 2 + core for d in range(1, halves)]
    return to, origin


def greet(halves, n_slab):
    slab, rep, _, _, partner = place()
    to, _ = peers_of(halves)
    targets = [(slab, partner)] + [(slab, peer) for peer in to]
    targets += [(slab_at(d), rep) for d in range(1, n_slab)]
    barrier = pltpu.get_barrier_semaphore()
    for target in targets:
        pl.semaphore_signal(barrier, inc=1, device_id=target, device_id_type=pl.DeviceIdType.MESH)
    return lambda: pl.semaphore_wait(barrier, len(targets))


def column(row):
    return jnp.broadcast_to(row, (LANES, row.shape[1])).T


def link_entries(row, live):
    n = row.shape[1]
    keys = column(row)
    at = lax.broadcasted_iota(i32, (n, LANES), 0)
    lane = lax.broadcasted_iota(i32, (n, LANES), 1)
    prev = []
    for p in range(n // LANES):
        same = (keys == row[:, p * LANES : (p + 1) * LANES]) & (at < lane + p * LANES)
        prev.append(jnp.max(jnp.where(same, at + 1, 0), axis=0, keepdims=True))
    last = jnp.max(jnp.where((keys == lane) & (at < live), at + 1, 0), axis=0, keepdims=True)
    return jnp.concatenate(prev, axis=1), last


def turn_of(slot):
    g = slot // SLOT_CAP
    pos = jnp.zeros_like(slot)
    for p, which in enumerate(TURNS):
        pos = jnp.where(g == which, p, pos)
    return pos * SLOT_CAP + (slot - g * SLOT_CAP)


def link_arrivals(slot_block, halves):
    _, _, core, half, _ = place()
    slots = NEIGH * SLOT_CAP
    per_core, per_rep = SLOT_CAP // 2, SLOT_CAP // (2 * halves)
    lane = lax.broadcasted_iota(i32, (1, slots), 1)
    row = jnp.zeros((1, slots), i32)
    for g in range(NEIGH):
        mine = slot_block[pl.ds(slab_at(MID - g), 1), :]
        row = jnp.where(lane // SLOT_CAP == g, mine, row)
    row = jnp.concatenate([row, jnp.full((1, LANES - slots), -1, i32)], axis=1)
    keys = column(row)
    slot = lax.broadcasted_iota(i32, (LANES, LANES), 0)
    lane = lax.broadcasted_iota(i32, (LANES, LANES), 1)
    g, k = slot // SLOT_CAP, slot % SLOT_CAP
    of_core = k // per_core == core
    of_rep = of_core & (k % per_core // per_rep == half)
    held = of_rep | (g == MID)
    for d in DIRECT:
        held = held | (of_core & (g == d))
    order_c, order_r = turn_of(slot), turn_of(lane)
    prev = jnp.max(
        jnp.where((keys == row) & held & (order_c < order_r), order_c + 1, 0), axis=0, keepdims=True
    )
    last = jnp.max(jnp.where((keys == lane) & held, order_c + 1, 0), axis=0, keepdims=True)
    return prev, last


def run_edges(n, product, prev, hist, midway=None):
    unroll = math.gcd(n, EDGE_UNROLL)
    turns = n // unroll

    def turn(i, carry):
        work = [product(i * unroll + u) for u in range(unroll)]
        for u, term in enumerate(work):
            e = i * unroll + u
            hist[e + 1] = hist[prev(e)] + term
        return carry

    if midway is None:
        lax.fori_loop(0, turns, turn, 0)
    else:
        lax.fori_loop(0, turns // 2, turn, 0)
        midway()
        lax.fori_loop(turns // 2, turns, turn, 0)


def share(wires, halves, per_rep, arrived, old, ready, beside):
    slab, _, core, half, partner = place()
    to, _ = peers_of(halves)
    across, on = {}, []
    wires.flush(old)

    def part(g, h, n):
        return arrived.at[pl.ds(g * SLOT_CAP + (core * halves + h) * per_rep, n * per_rep)]

    def pass_on(g):
        for d in range(1, halves):
            across[g][d - 1].wait_recv()
            theirs = part(g, lax.rem(half + halves - d, halves), 1)
            on.append(wires.send(theirs, theirs, slab, partner))

    for g in DIRECT_B:
        ready(g)
        on.append(wires.send(part(g, 0, halves), part(g, 0, halves), slab, partner))
    for i in range(len(FOLDED_B) + LAG):
        if i < len(FOLDED_B):
            g = FOLDED_B[i]
            ready(g)
            own = part(g, half, 1)
            across[g] = [wires.send(own, own, slab, peer) for peer in to]
            on.append(wires.send(own, own, slab, partner))
        for at, work in beside:
            if at == i:
                work()
        if i >= LAG:
            pass_on(FOLDED_B[i - LAG])
    for copy in on:
        copy.wait_recv()


def fold(wires, halves, starts, step, block_sum, bufs, finish):
    slab, _, core, half, partner = place()
    part, from_core, to_far, from_far = bufs
    near, far = {}, {}
    old = len(wires.sending)

    def over_cores(d):
        h = lax.rem(half + d, halves)
        for b0 in starts:
            for b in range(b0, b0 + step):
                part[d, b] = block_sum(h, 1 - core, b).astype(bf16)
            at = pl.ds(b0, step)
            near[d, b0] = wires.send(part.at[d, at], from_core.at[d, at], slab, partner)

    for d in range(1, halves):
        over_cores(d)
    for d in range(1, halves):
        h = lax.rem(half + d, halves)
        for b0 in starts:
            near[d, b0].wait_recv()
            for b in range(b0, b0 + step):
                to_far[d - 1, b] = (block_sum(h, core, b) + from_core[d, b].astype(f32)).astype(bf16)
            at = pl.ds(b0, step)
            far[d, b0] = wires.send(to_far.at[d - 1, at], from_far.at[d - 1, at], slab, h * 2 + core)
    over_cores(0)
    wires.flush(old)
    for b0 in starts:
        near[0, b0].wait_recv()
        ours = [block_sum(half, core, b) + from_core[0, b].astype(f32) for b in range(b0, b0 + step)]
        for d in range(1, halves):
            far[d, b0].wait_recv()
            ours = [total + from_far[d - 1, b0 + i].astype(f32) for i, total in enumerate(ours)]
        finish(b0, ours)


def layer_kernel(
    halves,
    n_slab,
    each,
    feats_hbm,
    cot_hbm,
    table_hbm,
    srcs_hbm,
    tiles_hbm,
    slots_hbm,
    count_hbm,
    slot_block_hbm,
    gain_hbm,
    w_in_hbm,
    b_in_hbm,
    w_out_hbm,
    updated_hbm,
    grad_feats_hbm,
    grads_hbm,
    cot,
    src_v,
    slot_v,
    srcs,
    tiles,
    slots,
    count,
    slot_block_v,
    slot_block,
    gain,
    w_in,
    b_in,
    w_out,
    updated,
    grad_feats,
    grads,
    table,
    slab_feats,
    meta_v,
    meta,
    hist,
    part,
    from_core,
    to_far,
    from_far,
    outgoing,
    arrived,
    agg_hist,
    a_part,
    a_core,
    a_to,
    a_far,
    normed_s,
    act_s,
    d_pre_s,
    d_own,
    gathered,
    out_b,
    arrived_b,
    packed,
    w_core,
    w_to,
    w_far,
    w_rep,
    w_pieces,
    w_piece,
    e_part,
    e_core,
    e_to,
    e_far,
    local_sems,
    send_sems,
    recv_sems,
):
    slab, rep, core, half, partner = place()
    to, origin = peers_of(halves)
    wires = Wires(send_sems, recv_sems)
    nb, rows_b, width = d_own.shape
    n_rep = 2 * halves
    per_rep = SLOT_CAP // n_rep
    entries = srcs.shape[1]
    peers = range(1, n_slab)

    arrive = greet(halves, n_slab)
    own = slab_feats.at[pl.ds(rep * nb, nb)]
    loads = [
        pltpu.make_async_copy(src, dst, local_sems.at[i])
        for i, (src, dst) in enumerate(
            [
                (slots_hbm, slot_v),
                (srcs_hbm, src_v),
                (slot_block_hbm, slot_block_v),
                (count_hbm, count),
                (feats_hbm, own),
                (srcs_hbm, srcs),
                (tiles_hbm, tiles),
                (slots_hbm, slots),
                (slot_block_hbm, slot_block),
                (table_hbm, table),
                (cot_hbm, cot),
                (gain_hbm, gain),
                (w_in_hbm, w_in),
                (b_in_hbm, b_in),
                (w_out_hbm, w_out),
            ]
        )
    ]
    local_used = len(loads)
    for load in loads:
        load.start()
    arrive()
    loads[4].wait()

    def blocks(ref, who, at, n):
        return ref.at[pl.ds(who * nb + at, n)]

    def gather_begin(mine, out, at, n):
        src = mine.at[pl.ds(at, n)]
        far = [wires.send(src, blocks(out, rep, at, n), slab, peer) for peer in to]
        near = wires.send(src, blocks(out, rep, at, n), slab, partner)
        return far, near

    def gather_forward(begun, out, at, n):
        onward = [begun[1]]
        for copy, who in zip(begun[0], origin):
            copy.wait_recv()
            ref = blocks(out, who, at, n)
            onward.append(wires.send(ref, ref, slab, partner))
        return onward

    step = nb // PIECES if nb % PIECES == 0 else nb
    starts = list(range(0, nb, step))
    begun = [gather_begin(own, slab_feats, at, step) for at in starts]
    for load in loads[:4]:
        load.wait()

    meta_v[...] = jnp.zeros_like(meta_v)
    prev, last = link_entries(slot_v[...], count[0])
    meta_v[PREV_F : PREV_F + 1, :] = prev
    meta_v[LAST_F : LAST_F + 1, 0:LANES] = last
    prev, last = link_entries(src_v[...], count[0])
    meta_v[PREV_B : PREV_B + 1, :] = prev
    meta_v[LAST_B : LAST_B + 1, 0:LANES] = last
    prev, last = link_arrivals(slot_block_v, halves)
    meta_v[PREV_A : PREV_A + 1, 0:LANES] = prev
    meta_v[LAST_A : LAST_A + 1, 0:LANES] = last
    known = pltpu.make_async_copy(meta_v, meta, local_sems.at[local_used])
    known.start()
    hist[0] = jnp.zeros((rows_b, width), f32)
    agg_hist[0] = jnp.zeros((rows_b, width), f32)
    known.wait()
    for load in loads[5:]:
        load.wait()
    onward = []
    for at, b in zip(starts, begun):
        onward += gather_forward(b, slab_feats, at, step)
    for copy in onward:
        copy.wait_recv()

    run_edges(
        entries,
        lambda e: jnp.dot(table[tiles[0, e]], slab_feats[srcs[0, e]], preferred_element_type=f32),
        lambda e: meta[PREV_F, e],
        hist,
    )

    def slot_sum(g, c, h, j):
        slot = g * SLOT_CAP + (c * halves + h) * per_rep + j
        return hist[meta[LAST_F, slot]]

    first, cross, second = {}, {}, {}
    for g in AWAY:
        for h in range(halves):
            for j in range(per_rep):
                part[g, h, j] = slot_sum(g, 1 - core, h, j).astype(bf16)
        first[g] = wires.send(part.at[g], from_core.at[g], slab, partner)

    def core_sum(g, h, j):
        return slot_sum(g, core, h, j) + from_core[g, h, j].astype(f32)

    for g in DIRECT:
        first[g].wait_recv()
        for h in range(halves):
            for j in range(per_rep):
                outgoing[g, h, j] = core_sum(g, h, j).astype(bf16)
        second[g] = wires.send(outgoing.at[g], arrived.at[g], slab_at(g - MID), rep)
    for g in FOLDED:
        first[g].wait_recv()
        cross[g] = []
        for d in range(1, halves):
            h = lax.rem(half + d, halves)
            for j in range(per_rep):
                to_far[d - 1, g, j] = core_sum(g, h, j).astype(bf16)
            cross[g].append(
                wires.send(to_far.at[d - 1, g], from_far.at[d - 1, g], slab, h * 2 + core)
            )
    for g in FOLDED:
        for copy in cross[g]:
            copy.wait_recv()
        for j in range(per_rep):
            total = core_sum(g, half, j)
            for d in range(1, halves):
                total = total + from_far[d - 1, g, j].astype(f32)
            outgoing[g, 0, j] = total.astype(bf16)
        second[g] = wires.send(outgoing.at[g, 0], arrived.at[g, 0], slab_at(g - MID), rep)

    def add_to(g, c, h, j, value):
        k = (c * halves + h) * per_rep + j
        at = TURNS.index(g) * SLOT_CAP + k
        agg_hist[at + 1] = agg_hist[meta[PREV_A, g * SLOT_CAP + k]] + value

    for c in range(2):
        for h in range(halves):
            for j in range(per_rep):
                add_to(MID, c, h, j, slot_sum(MID, c, h, j))
    for g in DIRECT:
        second[g].wait_recv()
        for h in range(halves):
            for j in range(per_rep):
                add_to(g, core, h, j, arrived[g, h, j].astype(f32))
    for g in FOLDED:
        second[g].wait_recv()
        for j in range(per_rep):
            add_to(g, core, half, j, arrived[g, 0, j].astype(f32))

    rows = step * rows_b
    g_gains, g_bs, begun = [], [], []

    def update_nodes(b0, totals):
        at = pl.ds(b0 * rows_b, rows)
        feat = own[pl.ds(b0, step)].reshape(rows, width).astype(f32)
        cots = cot[at]
        agg = jnp.concatenate(totals, axis=0)
        wide = jnp.concatenate([feat, agg], axis=1)
        inv = lax.rsqrt(jnp.mean(wide * wide, axis=1, keepdims=True) + RMS_EPS)
        scaled = wide * inv
        normed = (scaled * gain[...]).astype(bf16)
        pre = jnp.dot(normed, w_in[...], preferred_element_type=f32) + b_in[...]
        sg = jax.nn.sigmoid(pre)
        act = (pre * sg).astype(bf16)
        d_act = lax.dot_general(cots, w_out[...], (((1,), (1,)), ((), ())), preferred_element_type=f32)
        d_pre = d_act * sg * (1.0 + pre * (1.0 - sg))
        d_pre_b = d_pre.astype(bf16)
        d_normed = lax.dot_general(
            d_pre_b, w_in[...], (((1,), (1,)), ((), ())), preferred_element_type=f32
        )
        d_scaled = d_normed * gain[...]
        inner = jnp.mean(d_scaled * wide, axis=1, keepdims=True)
        d_wide = inv * d_scaled - inv * inv * inv * wide * inner
        for b in range(step):
            d_own[b0 + b] = d_wide[b * rows_b : (b + 1) * rows_b, width:].T.astype(bf16)
        begun.append(gather_begin(d_own, gathered, b0, step))
        grad_feats[at] = cots.astype(f32) + d_wide[:, :width]
        normed_s[at] = normed
        act_s[at] = act
        d_pre_s[at] = d_pre_b
        g_gains.append(jnp.sum(d_normed * scaled, axis=0, keepdims=True))
        g_bs.append(jnp.sum(d_pre, axis=0, keepdims=True))
        updated[at] = (feat + jnp.dot(act, w_out[...], preferred_element_type=f32)).astype(bf16)

    fold(
        wires,
        halves,
        starts,
        step,
        lambda h, c, b: agg_hist[meta[LAST_A, (h * 2 + c) * nb + b]],
        (a_part, a_core, a_to, a_far),
        update_nodes,
    )
    g_gain, g_b = sum(g_gains), sum(g_bs)
    gathered[pl.ds(rep * nb, nb)] = d_own[...]
    stores = [pltpu.make_async_copy(updated, updated_hbm, local_sems.at[local_used + 1])]
    stores[0].start()

    over_rows = (((0,), (0,)), ((), ()))
    n_in, hidden = w_in.shape
    panels = hidden // width

    def weights_in(c):
        panel = lax.dot_general(
            normed_s[...], d_pre_s[:, width * c : width * (c + 1)], over_rows, preferred_element_type=f32
        )
        packed[n_in * c : n_in * (c + 1)] = panel.astype(bf16)

    onward = []
    for at, b in zip(starts[:-1], begun[:-1]):
        onward += gather_forward(b, gathered, at, step)
    n = n_in * panels
    g_out = lax.dot_general(act_s[...], cot[...], over_rows, preferred_element_type=f32)
    packed[n : n + hidden] = g_out.astype(bf16)
    n += hidden
    rest = [
        value[:, width * c : width * (c + 1)]
        for value in (g_gain, g_b)
        for c in range(value.shape[1] // width)
    ]
    rest.append(jnp.zeros((16 - len(rest), width), f32))
    packed[n : n + 16] = jnp.concatenate(rest, axis=0).astype(bf16)
    n += 16
    if packed.shape[0] > n:
        packed[n:] = jnp.zeros((packed.shape[0] - n, width), bf16)
    onward += gather_forward(begun[-1], gathered, starts[-1], step)
    for c in range(panels):
        weights_in(c)
    for copy in onward:
        copy.wait_recv()

    def pick(g, c, h, j):
        dest = slot_block[slab_at(MID - g), g * SLOT_CAP + (c * halves + h) * per_rep + j]
        return gathered[dest]

    def slots_of(g, h, n):
        return arrived_b.at[pl.ds(g * SLOT_CAP + (core * halves + h) * per_rep, n * per_rep)]

    second_b = {}
    old = len(wires.sending)
    for g in DIRECT_B:
        for h in range(halves):
            for j in range(per_rep):
                out_b[g, h * per_rep + j] = pick(g, core, h, j)
        second_b[g] = wires.send(out_b.at[g], slots_of(g, 0, halves), slab_at(MID - g), rep)
    for g in FOLDED_B:
        for j in range(per_rep):
            out_b[g, j] = pick(g, core, half, j)
        second_b[g] = wires.send(
            out_b.at[g, pl.ds(0, per_rep)], slots_of(g, half, 1), slab_at(MID - g), rep
        )
    for c in range(2):
        for h in range(halves):
            for j in range(per_rep):
                arrived_b[MID * SLOT_CAP + (c * halves + h) * per_rep + j] = pick(MID, c, h, j)

    chunk = n_slab * each

    def of_rep(ref, h, c):
        return ref.at[pl.ds((h * 2 + c) * chunk, chunk)]

    near = []
    for d in list(range(1, halves)) + [0]:
        h = lax.rem(half + d, halves)
        near.append((d, h, wires.send(of_rep(packed, h, 1 - core), w_core.at[h], slab, partner)))
    w_cross = []
    for d, h, copy in near:
        copy.wait_recv()
        if d > 0:
            total = of_rep(packed, h, core)[...].astype(f32) + w_core[h].astype(f32)
            w_to[d - 1] = total.astype(bf16)
            w_cross.append(wires.send(w_to.at[d - 1], w_far.at[d - 1], slab, h * 2 + core))

    w_slab = []

    def scatter_weights():
        total = of_rep(packed, half, core)[...].astype(f32) + w_core[half].astype(f32)
        for d, copy in enumerate(w_cross):
            copy.wait_recv()
            total = total + w_far[d].astype(f32)
        w_rep[...] = total.astype(bf16)
        for d in peers:
            peer = slab_at(d)
            w_slab.append(
                wires.send(w_rep.at[pl.ds(peer * each, each)], w_pieces.at[d - 1], peer, rep)
            )

    w_back, w_far_g, w_on = [], [], []

    def collect_weights():
        total = w_rep[pl.ds(slab * each, each)].astype(f32)
        for d, copy in enumerate(w_slab):
            copy.wait_recv()
            total = total + w_pieces[d].astype(f32)
        w_piece[...] = total.astype(bf16)
        mine = grads.at[rep, pl.ds(slab * each, each)]
        mine[...] = w_piece[...]
        w_back.extend(wires.send(w_piece, mine, slab_at(d), rep) for d in peers)

    def spread_weights():
        for copy in w_back:
            copy.wait_recv()
        w_far_g.extend(wires.send(grads.at[rep], grads.at[rep], slab, peer) for peer in to)
        w_on.append(wires.send(grads.at[rep], grads.at[rep], slab, partner))

    share(
        wires,
        halves,
        per_rep,
        arrived_b,
        old,
        lambda g: second_b[g].wait_recv(),
        [(SCATTER_AT, scatter_weights), (COLLECT_AT, collect_weights)],
    )
    def product_b(e):
        return jnp.dot(arrived_b[slots[0, e]], table[tiles[0, e]], preferred_element_type=f32)

    run_edges(entries, product_b, lambda e: meta[PREV_B, e], hist, spread_weights)
    for copy, who in zip(w_far_g, origin):
        copy.wait_recv()
        w_on.append(wires.send(grads.at[who], grads.at[who], slab, partner))

    def block_sum(h, c, b):
        return hist[meta[LAST_B, (h * 2 + c) * nb + b]]

    def add_folded(b0, totals):
        if b0 == starts[-1]:
            for copy in w_on:
                copy.wait_recv()
            stores.append(pltpu.make_async_copy(grads, grads_hbm, local_sems.at[local_used + 2]))
            stores[-1].start()
        for b, total in enumerate(totals):
            at = pl.ds((b0 + b) * rows_b, rows_b)
            grad_feats[at] = grad_feats[at] + total.T
        at = pl.ds(b0 * rows_b, rows)
        store = pltpu.make_async_copy(
            grad_feats.at[at], grad_feats_hbm.at[at], local_sems.at[local_used + 3 + b0 // step]
        )
        store.start()
        stores.append(store)

    fold(
        wires, halves, starts, step, block_sum, (e_part, e_core, e_to, e_far), add_folded
    )
    wires.flush()
    for store in stores:
        store.wait()


def final_kernel(
    scale, updated_in, feats_in, grads_in, updated, grad_feats, g_gain, g_in, g_b, g_out,
    updated_v, feats_v, grads, gain_v, in_v, b_v, out_v, load_sems, store_sems,
):
    rows = feats_v.shape[0] // PIECES
    pieces = [pl.ds(i * rows, rows) for i in range(PIECES)]
    through = [(grads_in, grads, None)]
    through += [(feats_in.at[at], feats_v.at[at], grad_feats.at[at]) for at in pieces]
    through += [(updated_in, updated_v, updated)]
    loads = [
        pltpu.make_async_copy(src, held, load_sems.at[i]) for i, (src, held, _) in enumerate(through)
    ]
    stores = []

    def store(src, dst):
        stores.append(pltpu.make_async_copy(src, dst, store_sems.at[len(stores)]))
        stores[-1].start()

    for load in loads:
        load.start()
    width = grads.shape[1]

    def part(at, n):
        return grads[at : at + n].astype(f32) * scale

    loads[0].wait()
    n, panels = in_v.shape[0], in_v.shape[1] // width
    for c in range(panels):
        in_v[:, width * c : width * (c + 1)] = part(n * c, n)
    store(in_v, g_in)
    n = n * panels
    out_v[...] = part(n, out_v.shape[0])
    store(out_v, g_out)
    rest = part(n + out_v.shape[0], 16)
    at = 0
    for ref in (gain_v, b_v):
        for c in range(ref.shape[1] // width):
            ref[:, width * c : width * (c + 1)] = rest[at : at + 1]
            at += 1
    store(gain_v, g_gain)
    store(b_v, g_b)
    for load, (_, held, dst) in zip(loads[1:], through[1:]):
        load.wait()
        store(held, dst)
    for copy in stores:
        copy.wait()


def body(
    feats,
    cotangent,
    tile_table,
    edge_src,
    edge_tile,
    edge_slot,
    edge_count,
    slot_block,
    norm_gain,
    w_in,
    b_in,
    w_out,
):
    n_slab = lax.axis_size("slab")
    n_rep = lax.axis_size("rep")
    halves = n_rep // 2
    rows_dev, width = feats.shape
    hidden = w_out.shape[0]
    rows_b = tile_table.shape[1]
    nb = rows_dev // rows_b
    slab_blocks = nb * n_rep
    entries = edge_src.shape[1]
    per_rep = SLOT_CAP // n_rep
    used = w_in.size // width + hidden + 16
    each = -(-used // (n_slab * n_rep * 16)) * 16
    chunk = n_slab * each
    shape = jax.ShapeDtypeStruct
    n_sems = 224 + 2 * n_slab

    def block(*lead, dtype=bf16):
        return pltpu.VMEM((*lead, rows_b, width), dtype)

    def weights(*lead):
        return pltpu.VMEM((*lead, width), bf16)

    updated, grad_feats, grads = pl.pallas_call(
        functools.partial(layer_kernel, halves, n_slab, each),
        out_shape=(
            shape((rows_dev, width), bf16),
            shape((rows_dev, width), f32),
            shape((n_rep, chunk, width), bf16),
        ),
        in_specs=[ANY] * 12,
        out_specs=(ANY,) * 3,
        scratch_shapes=[
            pltpu.VMEM((rows_dev, width), bf16),
            pltpu.VMEM(edge_src.shape, i32),
            pltpu.VMEM(edge_slot.shape, i32),
            pltpu.SMEM(edge_src.shape, i32),
            pltpu.SMEM(edge_tile.shape, i32),
            pltpu.SMEM(edge_slot.shape, i32),
            pltpu.SMEM(edge_count.shape, i32),
            pltpu.VMEM(slot_block.shape, i32),
            pltpu.SMEM(slot_block.shape, i32),
            pltpu.VMEM((1, 2 * width), f32),
            pltpu.VMEM(w_in.shape, bf16),
            pltpu.VMEM((1, hidden), f32),
            pltpu.VMEM(w_out.shape, bf16),
            pltpu.VMEM((rows_dev, width), bf16),
            pltpu.VMEM((rows_dev, width), f32),
            weights(n_rep, chunk),
            pltpu.VMEM(tile_table.shape, bf16),
            block(slab_blocks),
            pltpu.VMEM((8, entries), i32),
            pltpu.SMEM((8, entries), i32),
            block(entries + 1, dtype=f32),
            block(NEIGH, halves, per_rep),
            block(NEIGH, halves, per_rep),
            block(halves - 1, NEIGH, per_rep),
            block(halves - 1, NEIGH, per_rep),
            block(NEIGH, halves, per_rep),
            block(NEIGH, halves, per_rep),
            block(NEIGH * SLOT_CAP + 1, dtype=f32),
            block(halves, nb),
            block(halves, nb),
            block(halves - 1, nb),
            block(halves - 1, nb),
            pltpu.VMEM((rows_dev, 2 * width), bf16),
            pltpu.VMEM((rows_dev, hidden), bf16),
            pltpu.VMEM((rows_dev, hidden), bf16),
            block(nb),
            block(slab_blocks),
            block(NEIGH, halves * per_rep),
            block(NEIGH * SLOT_CAP),
            weights(n_rep * chunk),
            weights(halves, chunk),
            weights(halves - 1, chunk),
            weights(halves - 1, chunk),
            weights(chunk),
            weights(n_slab - 1, each),
            weights(each),
            block(halves, nb),
            block(halves, nb),
            block(halves - 1, nb),
            block(halves - 1, nb),
            DMA((24 + PIECES,)),
            DMA((n_sems,)),
            DMA((n_sems,)),
        ],
        compiler_params=pltpu.CompilerParams(
            collective_id=0, has_side_effects=True, vmem_limit_bytes=58 << 20
        ),
    )(
        feats.reshape(nb, rows_b, width),
        cotangent,
        tile_table,
        edge_src,
        edge_tile,
        edge_slot,
        edge_count,
        slot_block,
        norm_gain.reshape(1, -1),
        w_in,
        b_in.reshape(1, -1),
        w_out,
    )
    scale = float(rows_dev * n_slab * n_rep) ** (-0.5)
    updated, grad_feats, grad_gain, grad_w_in, grad_b_in, grad_w_out = pl.pallas_call(
        functools.partial(final_kernel, scale),
        out_shape=(
            shape((rows_dev, width), bf16),
            shape((rows_dev, width), f32),
            shape((1, 2 * width), f32),
            shape(w_in.shape, f32),
            shape((1, hidden), f32),
            shape(w_out.shape, f32),
        ),
        in_specs=[ANY] * 3,
        out_specs=(ANY,) * 6,
        scratch_shapes=[
            pltpu.VMEM((rows_dev, width), bf16),
            pltpu.VMEM((rows_dev, width), f32),
            weights(n_rep * chunk),
            pltpu.VMEM((1, 2 * width), f32),
            pltpu.VMEM(w_in.shape, f32),
            pltpu.VMEM((1, hidden), f32),
            pltpu.VMEM(w_out.shape, f32),
            DMA((2 + PIECES,)),
            DMA((5 + PIECES,)),
        ],
    )(updated, grad_feats, grads.reshape(-1, width))
    return (
        updated,
        grad_feats,
        grad_gain.reshape(-1),
        grad_w_in,
        grad_b_in.reshape(-1),
        grad_w_out,
    )


def solution(mesh):
    rows = P(("slab", "rep"), None)
    placed = (rows, rows, P(("slab", "rep"), None, None)) + (rows,) * 3 + (P(("slab", "rep")),) + (P(),) * 5
    return jax.shard_map(
        body,
        mesh=mesh,
        in_specs=placed,
        out_specs=(rows, rows, P(), P(), P(), P()),
        check_vma=False,
    )
```

```python
import functools
import math

import jax
import jax.numpy as jnp
from jax import lax
from jax.experimental import pallas as pl
from jax.experimental.pallas import tpu as pltpu
from jax.sharding import PartitionSpec as P

NEIGH = 8
SLOT_CAP = 8
MID = NEIGH // 2

RMS_EPS = 1e-06
EDGE_UNROLL = 64
PIECES = 4
LANES = 128
VMEM = pl.BlockSpec(memory_space=pltpu.VMEM)
SMEM = pl.BlockSpec(memory_space=pltpu.SMEM)
ANY = pl.BlockSpec(memory_space=pl.ANY)
DMA = pltpu.SemaphoreType.DMA
DIRECT = [MID - 1, MID + 1]
FOLDED = sorted((g for g in range(NEIGH) if g != MID and g not in DIRECT), key=lambda g: abs(g - MID))
AWAY = DIRECT + FOLDED
TURNS = [MID] + AWAY
DIRECT_B = []
FOLDED_B = [g for g in sorted(range(NEIGH), key=lambda g: abs(g - MID)) if g != MID and g not in DIRECT_B]
LAG = 3
SCATTER_AT, COLLECT_AT = 2, 7
PREV_F, LAST_F, PREV_B, LAST_B, PREV_A, LAST_A = range(6)
f32, bf16, i32 = jnp.float32, jnp.bfloat16, jnp.int32


def place():
    slab, rep = lax.axis_index("slab"), lax.axis_index("rep")
    core = lax.rem(rep, 2)
    return slab, rep, core, lax.div(rep, 2), rep + 1 - 2 * core


def slab_at(offset):
    n_slab = lax.axis_size("slab")
    return lax.rem(lax.axis_index("slab") + offset + n_slab, n_slab)


class Wires:
    def __init__(self, send_sems, recv_sems):
        self.send_sems, self.recv_sems = send_sems, recv_sems
        self.used = 0
        self.sending = []

    def send(self, src, dst, slab, rep):
        copy = pltpu.make_async_remote_copy(
            src_ref=src,
            dst_ref=dst,
            send_sem=self.send_sems.at[self.used],
            recv_sem=self.recv_sems.at[self.used],
            device_id=(slab, rep),
            device_id_type=pl.DeviceIdType.MESH,
        )
        self.used += 1
        copy.start()
        self.sending.append(copy)
        return copy

    def flush(self, n=None):
        n = len(self.sending) if n is None else n
        for copy in self.sending[:n]:
            copy.wait_send()
        self.sending = self.sending[n:]


def peers_of(halves):
    _, _, core, half, _ = place()
    to = [lax.rem(half + d, halves) * 2 + core for d in range(1, halves)]
    origin = [lax.rem(half + halves - d, halves) * 2 + core for d in range(1, halves)]
    return to, origin


def greet(halves, n_slab):
    slab, rep, _, _, partner = place()
    to, _ = peers_of(halves)
    targets = [(slab, partner)] + [(slab, peer) for peer in to]
    targets += [(slab_at(d), rep) for d in range(1, n_slab)]
    barrier = pltpu.get_barrier_semaphore()
    for target in targets:
        pl.semaphore_signal(barrier, inc=1, device_id=target, device_id_type=pl.DeviceIdType.MESH)
    return lambda: pl.semaphore_wait(barrier, len(targets))


def column(row):
    return jnp.broadcast_to(row, (LANES, row.shape[1])).T


def link_entries(row, live):
    n = row.shape[1]
    keys = column(row)
    at = lax.broadcasted_iota(i32, (n, LANES), 0)
    lane = lax.broadcasted_iota(i32, (n, LANES), 1)
    prev = []
    for p in range(n // LANES):
        same = (keys == row[:, p * LANES : (p + 1) * LANES]) & (at < lane + p * LANES)
        prev.append(jnp.max(jnp.where(same, at + 1, 0), axis=0, keepdims=True))
    last = jnp.max(jnp.where((keys == lane) & (at < live), at + 1, 0), axis=0, keepdims=True)
    return jnp.concatenate(prev, axis=1), last


def turn_of(slot):
    g = slot // SLOT_CAP
    pos = jnp.zeros_like(slot)
    for p, which in enumerate(TURNS):
        pos = jnp.where(g == which, p, pos)
    return pos * SLOT_CAP + (slot - g * SLOT_CAP)


def link_arrivals(slot_block, halves):
    _, _, core, half, _ = place()
    slots = NEIGH * SLOT_CAP
    per_core, per_rep = SLOT_CAP // 2, SLOT_CAP // (2 * halves)
    lane = lax.broadcasted_iota(i32, (1, slots), 1)
    row = jnp.zeros((1, slots), i32)
    for g in range(NEIGH):
        mine = slot_block[pl.ds(slab_at(MID - g), 1), :]
        row = jnp.where(lane // SLOT_CAP == g, mine, row)
    row = jnp.concatenate([row, jnp.full((1, LANES - slots), -1, i32)], axis=1)
    keys = column(row)
    slot = lax.broadcasted_iota(i32, (LANES, LANES), 0)
    lane = lax.broadcasted_iota(i32, (LANES, LANES), 1)
    g, k = slot // SLOT_CAP, slot % SLOT_CAP
    of_core = k // per_core == core
    of_rep = of_core & (k % per_core // per_rep == half)
    held = of_rep | (g == MID)
    for d in DIRECT:
        held = held | (of_core & (g == d))
    order_c, order_r = turn_of(slot), turn_of(lane)
    prev = jnp.max(
        jnp.where((keys == row) & held & (order_c < order_r), order_c + 1, 0), axis=0, keepdims=True
    )
    last = jnp.max(jnp.where((keys == lane) & held, order_c + 1, 0), axis=0, keepdims=True)
    return prev, last


def run_edges(n, product, prev, hist, midway=None):
    unroll = math.gcd(n, EDGE_UNROLL)
    turns = n // unroll

    def turn(i, carry):
        work = [product(i * unroll + u) for u in range(unroll)]
        for u, term in enumerate(work):
            e = i * unroll + u
            hist[e + 1] = hist[prev(e)] + term
        return carry

    if midway is None:
        lax.fori_loop(0, turns, turn, 0)
    else:
        lax.fori_loop(0, turns // 2, turn, 0)
        midway()
        lax.fori_loop(turns // 2, turns, turn, 0)


def share(wires, halves, per_rep, arrived, old, ready, beside):
    slab, _, core, half, partner = place()
    to, _ = peers_of(halves)
    across, on = {}, []
    wires.flush(old)

    def part(g, h, n):
        return arrived.at[pl.ds(g * SLOT_CAP + (core * halves + h) * per_rep, n * per_rep)]

    def pass_on(g):
        for d in range(1, halves):
            across[g][d - 1].wait_recv()
            theirs = part(g, lax.rem(half + halves - d, halves), 1)
            on.append(wires.send(theirs, theirs, slab, partner))

    for g in DIRECT_B:
        ready(g)
        on.append(wires.send(part(g, 0, halves), part(g, 0, halves), slab, partner))
    for i in range(len(FOLDED_B) + LAG):
        if i < len(FOLDED_B):
            g = FOLDED_B[i]
            ready(g)
            own = part(g, half, 1)
            across[g] = [wires.send(own, own, slab, peer) for peer in to]
            on.append(wires.send(own, own, slab, partner))
        for at, work in beside:
            if at == i:
                work()
        if i >= LAG:
            pass_on(FOLDED_B[i - LAG])
    for copy in on:
        copy.wait_recv()


def fold(wires, halves, starts, step, block_sum, bufs, beside, finish):
    slab, _, core, half, partner = place()
    part, from_core, to_far, from_far = bufs
    near, far = {}, {}
    old = len(wires.sending)

    def over_cores(d):
        h = lax.rem(half + d, halves)
        for b0 in starts:
            for b in range(b0, b0 + step):
                part[d, b] = block_sum(h, 1 - core, b).astype(bf16)
            at = pl.ds(b0, step)
            near[d, b0] = wires.send(part.at[d, at], from_core.at[d, at], slab, partner)

    for d in range(1, halves):
        over_cores(d)
    for d in range(1, halves):
        h = lax.rem(half + d, halves)
        for b0 in starts:
            near[d, b0].wait_recv()
            for b in range(b0, b0 + step):
                to_far[d - 1, b] = (block_sum(h, core, b) + from_core[d, b].astype(f32)).astype(bf16)
            at = pl.ds(b0, step)
            far[d, b0] = wires.send(to_far.at[d - 1, at], from_far.at[d - 1, at], slab, h * 2 + core)
    over_cores(0)
    beside()
    wires.flush(old)
    for b0 in starts:
        near[0, b0].wait_recv()
        ours = [block_sum(half, core, b) + from_core[0, b].astype(f32) for b in range(b0, b0 + step)]
        for d in range(1, halves):
            far[d, b0].wait_recv()
            ours = [total + from_far[d - 1, b0 + i].astype(f32) for i, total in enumerate(ours)]
        finish(b0, ours)


def layer_kernel(
    halves,
    n_slab,
    each,
    feats_hbm,
    cot_hbm,
    table_hbm,
    srcs_hbm,
    tiles_hbm,
    slots_hbm,
    count_hbm,
    slot_block_hbm,
    gain_hbm,
    w_in_hbm,
    b_in_hbm,
    w_out_hbm,
    updated_hbm,
    grad_feats_hbm,
    grads_hbm,
    cot,
    src_v,
    slot_v,
    srcs,
    tiles,
    slots,
    count,
    slot_block_v,
    slot_block,
    gain,
    w_in,
    b_in,
    w_out,
    updated,
    grad_feats,
    grads,
    table,
    slab_feats,
    meta_v,
    meta,
    hist,
    part,
    from_core,
    to_far,
    from_far,
    outgoing,
    arrived,
    agg_hist,
    a_part,
    a_core,
    a_to,
    a_far,
    normed_s,
    act_s,
    d_pre_s,
    d_act_s,
    d_own,
    gathered,
    out_b,
    arrived_b,
    packed,
    w_core,
    w_to,
    w_far,
    w_rep,
    w_pieces,
    w_piece,
    e_part,
    e_core,
    e_to,
    e_far,
    local_sems,
    send_sems,
    recv_sems,
):
    slab, rep, core, half, partner = place()
    to, origin = peers_of(halves)
    wires = Wires(send_sems, recv_sems)
    nb, rows_b, width = d_own.shape
    n_rep = 2 * halves
    per_rep = SLOT_CAP // n_rep
    entries = srcs.shape[1]
    peers = range(1, n_slab)

    arrive = greet(halves, n_slab)
    own = slab_feats.at[pl.ds(rep * nb, nb)]
    loads = [
        pltpu.make_async_copy(src, dst, local_sems.at[i])
        for i, (src, dst) in enumerate(
            [
                (slots_hbm, slot_v),
                (srcs_hbm, src_v),
                (slot_block_hbm, slot_block_v),
                (count_hbm, count),
                (feats_hbm, own),
                (srcs_hbm, srcs),
                (tiles_hbm, tiles),
                (slots_hbm, slots),
                (slot_block_hbm, slot_block),
                (table_hbm, table),
                (cot_hbm, cot),
                (gain_hbm, gain),
                (w_in_hbm, w_in),
                (b_in_hbm, b_in),
                (w_out_hbm, w_out),
            ]
        )
    ]
    local_used = len(loads)
    for load in loads:
        load.start()
    arrive()
    loads[4].wait()

    def blocks(ref, who, at, n):
        return ref.at[pl.ds(who * nb + at, n)]

    def gather_begin(mine, out, at, n):
        src = mine.at[pl.ds(at, n)]
        far = [wires.send(src, blocks(out, rep, at, n), slab, peer) for peer in to]
        near = wires.send(src, blocks(out, rep, at, n), slab, partner)
        return far, near

    def gather_forward(begun, out, at, n):
        onward = [begun[1]]
        for copy, who in zip(begun[0], origin):
            copy.wait_recv()
            ref = blocks(out, who, at, n)
            onward.append(wires.send(ref, ref, slab, partner))
        return onward

    step = nb // PIECES if nb % PIECES == 0 else nb
    starts = list(range(0, nb, step))
    begun = [gather_begin(own, slab_feats, at, step) for at in starts]
    for load in loads[:4]:
        load.wait()

    meta_v[...] = jnp.zeros_like(meta_v)
    prev, last = link_entries(slot_v[...], count[0])
    meta_v[PREV_F : PREV_F + 1, :] = prev
    meta_v[LAST_F : LAST_F + 1, 0:LANES] = last
    prev, last = link_entries(src_v[...], count[0])
    meta_v[PREV_B : PREV_B + 1, :] = prev
    meta_v[LAST_B : LAST_B + 1, 0:LANES] = last
    prev, last = link_arrivals(slot_block_v, halves)
    meta_v[PREV_A : PREV_A + 1, 0:LANES] = prev
    meta_v[LAST_A : LAST_A + 1, 0:LANES] = last
    known = pltpu.make_async_copy(meta_v, meta, local_sems.at[local_used])
    known.start()
    hist[0] = jnp.zeros((rows_b, width), f32)
    agg_hist[0] = jnp.zeros((rows_b, width), f32)
    known.wait()
    for load in loads[5:]:
        load.wait()
    onward = []
    for at, b in zip(starts, begun):
        onward += gather_forward(b, slab_feats, at, step)
    for copy in onward:
        copy.wait_recv()

    run_edges(
        entries,
        lambda e: jnp.dot(table[tiles[0, e]], slab_feats[srcs[0, e]], preferred_element_type=f32),
        lambda e: meta[PREV_F, e],
        hist,
    )

    def slot_sum(g, c, h, j):
        slot = g * SLOT_CAP + (c * halves + h) * per_rep + j
        return hist[meta[LAST_F, slot]]

    first, cross, second = {}, {}, {}
    for g in AWAY:
        for h in range(halves):
            for j in range(per_rep):
                part[g, h, j] = slot_sum(g, 1 - core, h, j).astype(bf16)
        first[g] = wires.send(part.at[g], from_core.at[g], slab, partner)

    def core_sum(g, h, j):
        return slot_sum(g, core, h, j) + from_core[g, h, j].astype(f32)

    for g in DIRECT:
        first[g].wait_recv()
        for h in range(halves):
            for j in range(per_rep):
                outgoing[g, h, j] = core_sum(g, h, j).astype(bf16)
        second[g] = wires.send(outgoing.at[g], arrived.at[g], slab_at(g - MID), rep)
    for g in FOLDED:
        first[g].wait_recv()
        cross[g] = []
        for d in range(1, halves):
            h = lax.rem(half + d, halves)
            for j in range(per_rep):
                to_far[d - 1, g, j] = core_sum(g, h, j).astype(bf16)
            cross[g].append(
                wires.send(to_far.at[d - 1, g], from_far.at[d - 1, g], slab, h * 2 + core)
            )
    for g in FOLDED:
        for copy in cross[g]:
            copy.wait_recv()
        for j in range(per_rep):
            total = core_sum(g, half, j)
            for d in range(1, halves):
                total = total + from_far[d - 1, g, j].astype(f32)
            outgoing[g, 0, j] = total.astype(bf16)
        second[g] = wires.send(outgoing.at[g, 0], arrived.at[g, 0], slab_at(g - MID), rep)

    def add_to(g, c, h, j, value):
        k = (c * halves + h) * per_rep + j
        at = TURNS.index(g) * SLOT_CAP + k
        agg_hist[at + 1] = agg_hist[meta[PREV_A, g * SLOT_CAP + k]] + value

    for c in range(2):
        for h in range(halves):
            for j in range(per_rep):
                add_to(MID, c, h, j, slot_sum(MID, c, h, j))
    for g in DIRECT:
        second[g].wait_recv()
        for h in range(halves):
            for j in range(per_rep):
                add_to(g, core, h, j, arrived[g, h, j].astype(f32))
    for g in FOLDED:
        second[g].wait_recv()
        for j in range(per_rep):
            add_to(g, core, half, j, arrived[g, 0, j].astype(f32))

    rows = step * rows_b
    g_gains, g_bs, begun = [], [], []

    def begin_backward():
        for b0 in starts:
            at = pl.ds(b0 * rows_b, rows)
            d_act_s[at] = lax.dot_general(
                cot[at], w_out[...], (((1,), (1,)), ((), ())), preferred_element_type=f32
            )

    def update_nodes(b0, totals):
        at = pl.ds(b0 * rows_b, rows)
        feat = own[pl.ds(b0, step)].reshape(rows, width).astype(f32)
        cots = cot[at]
        agg = jnp.concatenate(totals, axis=0)
        wide = jnp.concatenate([feat, agg], axis=1)
        inv = lax.rsqrt(jnp.mean(wide * wide, axis=1, keepdims=True) + RMS_EPS)
        scaled = wide * inv
        normed = (scaled * gain[...]).astype(bf16)
        pre = jnp.dot(normed, w_in[...], preferred_element_type=f32) + b_in[...]
        sg = jax.nn.sigmoid(pre)
        act = (pre * sg).astype(bf16)
        d_act = d_act_s[at]
        d_pre = d_act * sg * (1.0 + pre * (1.0 - sg))
        d_pre_b = d_pre.astype(bf16)
        d_normed = lax.dot_general(
            d_pre_b, w_in[...], (((1,), (1,)), ((), ())), preferred_element_type=f32
        )
        d_scaled = d_normed * gain[...]
        inner = jnp.mean(d_scaled * wide, axis=1, keepdims=True)
        d_wide = inv * d_scaled - inv * inv * inv * wide * inner
        for b in range(step):
            d_own[b0 + b] = d_wide[b * rows_b : (b + 1) * rows_b, width:].T.astype(bf16)
        begun.append(gather_begin(d_own, gathered, b0, step))
        grad_feats[at] = cots.astype(f32) + d_wide[:, :width]
        normed_s[at] = normed
        act_s[at] = act
        d_pre_s[at] = d_pre_b
        g_gains.append(jnp.sum(d_normed * scaled, axis=0, keepdims=True))
        g_bs.append(jnp.sum(d_pre, axis=0, keepdims=True))
        updated[at] = (feat + jnp.dot(act, w_out[...], preferred_element_type=f32)).astype(bf16)

    fold(
        wires,
        halves,
        starts,
        step,
        lambda h, c, b: agg_hist[meta[LAST_A, (h * 2 + c) * nb + b]],
        (a_part, a_core, a_to, a_far),
        begin_backward,
        update_nodes,
    )
    g_gain, g_b = sum(g_gains), sum(g_bs)
    gathered[pl.ds(rep * nb, nb)] = d_own[...]
    stores = [pltpu.make_async_copy(updated, updated_hbm, local_sems.at[local_used + 1])]
    stores[0].start()

    over_rows = (((0,), (0,)), ((), ()))
    n_in, hidden = w_in.shape
    panels = hidden // width

    def weights_in(c):
        panel = lax.dot_general(
            normed_s[...], d_pre_s[:, width * c : width * (c + 1)], over_rows, preferred_element_type=f32
        )
        packed[n_in * c : n_in * (c + 1)] = panel.astype(bf16)

    onward = []
    for at, b in zip(starts[:-1], begun[:-1]):
        onward += gather_forward(b, gathered, at, step)
    n = n_in * panels
    g_out = lax.dot_general(act_s[...], cot[...], over_rows, preferred_element_type=f32)
    packed[n : n + hidden] = g_out.astype(bf16)
    n += hidden
    rest = [
        value[:, width * c : width * (c + 1)]
        for value in (g_gain, g_b)
        for c in range(value.shape[1] // width)
    ]
    rest.append(jnp.zeros((16 - len(rest), width), f32))
    packed[n : n + 16] = jnp.concatenate(rest, axis=0).astype(bf16)
    n += 16
    if packed.shape[0] > n:
        packed[n:] = jnp.zeros((packed.shape[0] - n, width), bf16)
    onward += gather_forward(begun[-1], gathered, starts[-1], step)
    for c in range(panels):
        weights_in(c)
    chunk = n_slab * each

    def of_rep(ref, h, c):
        return ref.at[pl.ds((h * 2 + c) * chunk, chunk)]

    near = []
    for d in list(range(1, halves)) + [0]:
        h = lax.rem(half + d, halves)
        near.append((d, h, wires.send(of_rep(packed, h, 1 - core), w_core.at[h], slab, partner)))
    for copy in onward:
        copy.wait_recv()

    def pick(g, c, h, j):
        dest = slot_block[slab_at(MID - g), g * SLOT_CAP + (c * halves + h) * per_rep + j]
        return gathered[dest]

    def slots_of(g, h, n):
        return arrived_b.at[pl.ds(g * SLOT_CAP + (core * halves + h) * per_rep, n * per_rep)]

    second_b = {}
    old = len(wires.sending)
    for g in DIRECT_B:
        for h in range(halves):
            for j in range(per_rep):
                out_b[g, h * per_rep + j] = pick(g, core, h, j)
        second_b[g] = wires.send(out_b.at[g], slots_of(g, 0, halves), slab_at(MID - g), rep)
    for g in FOLDED_B:
        for j in range(per_rep):
            out_b[g, j] = pick(g, core, half, j)
        second_b[g] = wires.send(
            out_b.at[g, pl.ds(0, per_rep)], slots_of(g, half, 1), slab_at(MID - g), rep
        )
    for c in range(2):
        for h in range(halves):
            for j in range(per_rep):
                arrived_b[MID * SLOT_CAP + (c * halves + h) * per_rep + j] = pick(MID, c, h, j)

    w_cross = []
    for d, h, copy in near:
        copy.wait_recv()
        if d > 0:
            total = of_rep(packed, h, core)[...].astype(f32) + w_core[h].astype(f32)
            w_to[d - 1] = total.astype(bf16)
            w_cross.append(wires.send(w_to.at[d - 1], w_far.at[d - 1], slab, h * 2 + core))

    w_slab = []

    def scatter_weights():
        total = of_rep(packed, half, core)[...].astype(f32) + w_core[half].astype(f32)
        for d, copy in enumerate(w_cross):
            copy.wait_recv()
            total = total + w_far[d].astype(f32)
        w_rep[...] = total.astype(bf16)
        for d in peers:
            peer = slab_at(d)
            w_slab.append(
                wires.send(w_rep.at[pl.ds(peer * each, each)], w_pieces.at[d - 1], peer, rep)
            )

    w_back, w_far_g, w_on = [], [], []

    def collect_weights():
        total = w_rep[pl.ds(slab * each, each)].astype(f32)
        for d, copy in enumerate(w_slab):
            copy.wait_recv()
            total = total + w_pieces[d].astype(f32)
        w_piece[...] = total.astype(bf16)
        mine = grads.at[rep, pl.ds(slab * each, each)]
        mine[...] = w_piece[...]
        w_back.extend(wires.send(w_piece, mine, slab_at(d), rep) for d in peers)

    def spread_weights():
        for copy in w_back:
            copy.wait_recv()
        w_far_g.extend(wires.send(grads.at[rep], grads.at[rep], slab, peer) for peer in to)
        w_on.append(wires.send(grads.at[rep], grads.at[rep], slab, partner))

    share(
        wires,
        halves,
        per_rep,
        arrived_b,
        old,
        lambda g: second_b[g].wait_recv(),
        [(SCATTER_AT, scatter_weights), (COLLECT_AT, collect_weights)],
    )
    def product_b(e):
        return jnp.dot(arrived_b[slots[0, e]], table[tiles[0, e]], preferred_element_type=f32)

    run_edges(entries, product_b, lambda e: meta[PREV_B, e], hist, spread_weights)
    for copy, who in zip(w_far_g, origin):
        copy.wait_recv()
        w_on.append(wires.send(grads.at[who], grads.at[who], slab, partner))

    def block_sum(h, c, b):
        return hist[meta[LAST_B, (h * 2 + c) * nb + b]]

    def add_folded(b0, totals):
        if b0 == starts[-1]:
            for copy in w_on:
                copy.wait_recv()
            stores.append(pltpu.make_async_copy(grads, grads_hbm, local_sems.at[local_used + 2]))
            stores[-1].start()
        for b, total in enumerate(totals):
            at = pl.ds((b0 + b) * rows_b, rows_b)
            grad_feats[at] = grad_feats[at] + total.T
        at = pl.ds(b0 * rows_b, rows)
        store = pltpu.make_async_copy(
            grad_feats.at[at], grad_feats_hbm.at[at], local_sems.at[local_used + 3 + b0 // step]
        )
        store.start()
        stores.append(store)

    fold(
        wires, halves, starts, step, block_sum, (e_part, e_core, e_to, e_far), lambda: None, add_folded
    )
    wires.flush()
    for store in stores:
        store.wait()


def final_kernel(
    scale, updated_in, feats_in, grads_in, updated, grad_feats, g_gain, g_in, g_b, g_out,
    updated_v, feats_v, grads, gain_v, in_v, b_v, out_v, load_sems, store_sems,
):
    rows = feats_v.shape[0] // PIECES
    pieces = [pl.ds(i * rows, rows) for i in range(PIECES)]
    through = [(grads_in, grads, None)]
    through += [(feats_in.at[at], feats_v.at[at], grad_feats.at[at]) for at in pieces]
    through += [(updated_in, updated_v, updated)]
    loads = [
        pltpu.make_async_copy(src, held, load_sems.at[i]) for i, (src, held, _) in enumerate(through)
    ]
    stores = []

    def store(src, dst):
        stores.append(pltpu.make_async_copy(src, dst, store_sems.at[len(stores)]))
        stores[-1].start()

    for load in loads:
        load.start()
    width = grads.shape[1]

    def part(at, n):
        return grads[at : at + n].astype(f32) * scale

    loads[0].wait()
    n, panels = in_v.shape[0], in_v.shape[1] // width
    for c in range(panels):
        in_v[:, width * c : width * (c + 1)] = part(n * c, n)
    store(in_v, g_in)
    n = n * panels
    out_v[...] = part(n, out_v.shape[0])
    store(out_v, g_out)
    rest = part(n + out_v.shape[0], 16)
    at = 0
    for ref in (gain_v, b_v):
        for c in range(ref.shape[1] // width):
            ref[:, width * c : width * (c + 1)] = rest[at : at + 1]
            at += 1
    store(gain_v, g_gain)
    store(b_v, g_b)
    for load, (_, held, dst) in zip(loads[1:], through[1:]):
        load.wait()
        store(held, dst)
    for copy in stores:
        copy.wait()


def body(
    feats,
    cotangent,
    tile_table,
    edge_src,
    edge_tile,
    edge_slot,
    edge_count,
    slot_block,
    norm_gain,
    w_in,
    b_in,
    w_out,
):
    n_slab = lax.axis_size("slab")
    n_rep = lax.axis_size("rep")
    halves = n_rep // 2
    rows_dev, width = feats.shape
    hidden = w_out.shape[0]
    rows_b = tile_table.shape[1]
    nb = rows_dev // rows_b
    slab_blocks = nb * n_rep
    entries = edge_src.shape[1]
    per_rep = SLOT_CAP // n_rep
    used = w_in.size // width + hidden + 16
    each = -(-used // (n_slab * n_rep * 16)) * 16
    chunk = n_slab * each
    shape = jax.ShapeDtypeStruct
    n_sems = 224 + 2 * n_slab

    def block(*lead, dtype=bf16):
        return pltpu.VMEM((*lead, rows_b, width), dtype)

    def weights(*lead):
        return pltpu.VMEM((*lead, width), bf16)

    updated, grad_feats, grads = pl.pallas_call(
        functools.partial(layer_kernel, halves, n_slab, each),
        out_shape=(
            shape((rows_dev, width), bf16),
            shape((rows_dev, width), f32),
            shape((n_rep, chunk, width), bf16),
        ),
        in_specs=[ANY] * 12,
        out_specs=(ANY,) * 3,
        scratch_shapes=[
            pltpu.VMEM((rows_dev, width), bf16),
            pltpu.VMEM(edge_src.shape, i32),
            pltpu.VMEM(edge_slot.shape, i32),
            pltpu.SMEM(edge_src.shape, i32),
            pltpu.SMEM(edge_tile.shape, i32),
            pltpu.SMEM(edge_slot.shape, i32),
            pltpu.SMEM(edge_count.shape, i32),
            pltpu.VMEM(slot_block.shape, i32),
            pltpu.SMEM(slot_block.shape, i32),
            pltpu.VMEM((1, 2 * width), f32),
            pltpu.VMEM(w_in.shape, bf16),
            pltpu.VMEM((1, hidden), f32),
            pltpu.VMEM(w_out.shape, bf16),
            pltpu.VMEM((rows_dev, width), bf16),
            pltpu.VMEM((rows_dev, width), f32),
            weights(n_rep, chunk),
            pltpu.VMEM(tile_table.shape, bf16),
            block(slab_blocks),
            pltpu.VMEM((8, entries), i32),
            pltpu.SMEM((8, entries), i32),
            block(entries + 1, dtype=f32),
            block(NEIGH, halves, per_rep),
            block(NEIGH, halves, per_rep),
            block(halves - 1, NEIGH, per_rep),
            block(halves - 1, NEIGH, per_rep),
            block(NEIGH, halves, per_rep),
            block(NEIGH, halves, per_rep),
            block(NEIGH * SLOT_CAP + 1, dtype=f32),
            block(halves, nb),
            block(halves, nb),
            block(halves - 1, nb),
            block(halves - 1, nb),
            pltpu.VMEM((rows_dev, 2 * width), bf16),
            pltpu.VMEM((rows_dev, hidden), bf16),
            pltpu.VMEM((rows_dev, hidden), bf16),
            pltpu.VMEM((rows_dev, hidden), f32),
            block(nb),
            block(slab_blocks),
            block(NEIGH, halves * per_rep),
            block(NEIGH * SLOT_CAP),
            weights(n_rep * chunk),
            weights(halves, chunk),
            weights(halves - 1, chunk),
            weights(halves - 1, chunk),
            weights(chunk),
            weights(n_slab - 1, each),
            weights(each),
            block(halves, nb),
            block(halves, nb),
            block(halves - 1, nb),
            block(halves - 1, nb),
            DMA((24 + PIECES,)),
            DMA((n_sems,)),
            DMA((n_sems,)),
        ],
        compiler_params=pltpu.CompilerParams(
            collective_id=0, has_side_effects=True, vmem_limit_bytes=58 << 20
        ),
    )(
        feats.reshape(nb, rows_b, width),
        cotangent,
        tile_table,
        edge_src,
        edge_tile,
        edge_slot,
        edge_count,
        slot_block,
        norm_gain.reshape(1, -1),
        w_in,
        b_in.reshape(1, -1),
        w_out,
    )
    scale = float(rows_dev * n_slab * n_rep) ** (-0.5)
    updated, grad_feats, grad_gain, grad_w_in, grad_b_in, grad_w_out = pl.pallas_call(
        functools.partial(final_kernel, scale),
        out_shape=(
            shape((rows_dev, width), bf16),
            shape((rows_dev, width), f32),
            shape((1, 2 * width), f32),
            shape(w_in.shape, f32),
            shape((1, hidden), f32),
            shape(w_out.shape, f32),
        ),
        in_specs=[ANY] * 3,
        out_specs=(ANY,) * 6,
        scratch_shapes=[
            pltpu.VMEM((rows_dev, width), bf16),
            pltpu.VMEM((rows_dev, width), f32),
            weights(n_rep * chunk),
            pltpu.VMEM((1, 2 * width), f32),
            pltpu.VMEM(w_in.shape, f32),
            pltpu.VMEM((1, hidden), f32),
            pltpu.VMEM(w_out.shape, f32),
            DMA((2 + PIECES,)),
            DMA((5 + PIECES,)),
        ],
    )(updated, grad_feats, grads.reshape(-1, width))
    return (
        updated,
        grad_feats,
        grad_gain.reshape(-1),
        grad_w_in,
        grad_b_in.reshape(-1),
        grad_w_out,
    )


def solution(mesh):
    rows = P(("slab", "rep"), None)
    placed = (rows, rows, P(("slab", "rep"), None, None)) + (rows,) * 3 + (P(("slab", "rep")),) + (P(),) * 5
    return jax.shard_map(
        body,
        mesh=mesh,
        in_specs=placed,
        out_specs=(rows, rows, P(), P(), P(), P()),
        check_vma=False,
    )
```
